512 devices in a mesh: dp: 256 (over x, y, z), mp: 2 (over core).
Axes of the slice: x: 4, y: 4, z: 16, core: 2. Of those that a mesh axis runs over, the one named last changes fastest.
Arguments:
- embeddings: bfloat16 [786432, 1024], P('dp', 'mp'), may hold values from -24 to 24
- first_level: int32 [786432], P('dp'), may hold values from 0 to 16383, as said below
- second_level: int32 [16384, 1], P('dp'), may hold values from 0 to 1023
Outputs:
- first_centroids: bfloat16 [16384, 1024], P('dp', 'mp')
- second_centroids: bfloat16 [1024, 1024], P('dp', 'mp')
- scores: float32 [16384, 1024], P('dp', 'mp')
The draws below stay inside these ranges and needn't reach their ends.
Inputs may be any that keep to these rules, and one draw needn't show every extreme that they name: `first_level`: the rows i * 3072 to (i + 1) * 3072 - 1 are assigned only to level-one centroids numbered from ((i + j) mod 256) * 64, that is to the centroids (i + j) * 64 to (i + j + 1) * 64 - 1 taken modulo 16384, for j from 0 to 7; every level-one centroid has at least one row. `second_level`: every level-two centroid is named by at least one level-one centroid.
All inputs are finite; a program needn't handle non-finite values.
Results may differ from the reference program's by a relative error of at most 0.012.
Values may be sent and summed in bfloat16 or wider, within the bound.
A program may use at most 64 MiB of HBM per device.

```python
import jax
import jax.numpy as jnp
from jax import lax

D = 1024
CENT_DEV = 64
BAND = 8
K2 = 1024
R_DEV = 3072
K1 = 16384
ROWS = 786432
N_DP = 256


def draw_first_level(key, part):
    devices = ROWS // R_DEV
    key_offset, key_local, key_order = jax.random.split(jax.random.fold_in(key, 11), 3)
    offsets = jax.random.randint(key_offset, (devices, R_DEV), 0, BAND)
    locals_drawn = jax.random.randint(key_local, (devices, R_DEV), 0, CENT_DEV)
    positions = jnp.arange(R_DEV, dtype=jnp.int32)[None, :]
    covering = positions < CENT_DEV
    offsets = jnp.where(covering, positions % BAND, offsets)
    locals_drawn = jnp.where(covering, positions % CENT_DEV, locals_drawn)
    orders = jax.vmap(lambda single: jax.random.permutation(single, R_DEV))(jax.random.split(key_order, devices))
    offsets = jnp.take_along_axis(offsets, orders, axis=1)
    locals_drawn = jnp.take_along_axis(locals_drawn, orders, axis=1)
    owners = (jnp.arange(devices, dtype=jnp.int32)[:, None] + offsets) % devices
    return (owners * CENT_DEV + locals_drawn).reshape(ROWS).astype(jnp.int32)


def block_scale(key, dims, cuts, least, high):
    factor_of = 1.0
    for dim, parts in cuts:
        heights = jax.random.uniform(jax.random.fold_in(jax.random.fold_in(key, 6), dim), (parts,), jnp.float32, least / len(cuts), high / len(cuts))
        factor_of = factor_of * jnp.repeat(jnp.exp(heights), dims[dim] // parts).reshape((-1,) + (1,) * (len(dims) - 1 - dim))
    return factor_of


def picks_of(key, rows, count, top, lift):
    order = jax.random.permutation(jax.random.fold_in(key, 1), count)
    boost = order
    for power in range(3):
        boost = boost * boost // count
    boost = boost * lift // count
    chance = jax.random.randint(jax.random.fold_in(key, 2), (rows, count), 0, 4096) + boost
    holders = jax.random.permutation(jax.random.fold_in(key, 3), rows)[jnp.arange(count) % rows]
    chance = jnp.where(jnp.arange(rows)[:, None] == holders[None, :], 1 << 14, chance)
    score = chance * count + jnp.arange(count)
    return lax.top_k(score.astype(jnp.int32), top)[1].astype(jnp.int32)


def bell_draw(stream_key, extent, deviation, limit, pieces=(), kind=jnp.bfloat16):
    values = deviation * jax.random.normal(stream_key, extent, jnp.float32)
    if pieces:
        values = values * block_scale(stream_key, extent, pieces, -0.22, 0.18)
    return jnp.clip(values, -limit, limit).astype(kind)


def setup_inputs(seed: int = 0) -> dict:
    key_of = jax.random.split(jax.random.key(seed), 4)
    embeddings = bell_draw(key_of[0], (ROWS, D), 4.0, 24.0, ((0, 256), (1, 2)))
    first_level = draw_first_level(jax.random.fold_in(key_of[3], 71), 0)
    second_level = picks_of(key_of[2], K1, K2, 1, 8)
    return {"embeddings": embeddings, "first_level": first_level, "second_level": second_level}


def reference(embeddings, first_level, second_level):
    clusters = CENT_DEV * N_DP
    width = embeddings.shape[1]

    def accumulate(running, pair):
        rows_block, ids_block = pair
        totals = running[0] + jax.ops.segment_sum(rows_block.astype(jnp.float32), ids_block, num_segments=clusters)
        tallies = running[1] + jax.ops.segment_sum(jnp.ones(ids_block.shape, jnp.float32), ids_block, num_segments=clusters)
        return (totals, tallies), None

    start_state = (jnp.zeros((clusters, width), jnp.float32), jnp.zeros((clusters,), jnp.float32))
    (first_sums, first_counts), unused = lax.scan(
        accumulate, start_state,
        (embeddings.reshape(N_DP, R_DEV, width), first_level.reshape(N_DP, R_DEV)))
    first_centroids = (first_sums / first_counts[:, None]).astype(jnp.bfloat16)
    group_ids = second_level[:, 0]
    second_sums = jax.ops.segment_sum(first_centroids.astype(jnp.float32), group_ids, num_segments=K2)
    second_counts = jax.ops.segment_sum(jnp.ones(group_ids.shape, jnp.float32), group_ids, num_segments=K2)
    second_centroids = (second_sums / second_counts[:, None]).astype(jnp.bfloat16)
    values = second_centroids.astype(jnp.float32)
    products = jnp.dot(first_centroids, second_centroids.T, preferred_element_type=jnp.float32)
    scores = products - 0.5 * jnp.sum(values * values, axis=1)[None, :]
    return first_centroids, second_centroids, scores
```

```python
import jax
import jax.numpy as jnp
from jax import lax
from jax.experimental import pallas as pl
from jax.experimental.pallas import tpu as pltpu
from jax.sharding import Mesh
from jax.sharding import PartitionSpec as P

NX, NY, NZ = 4, 4, 16
CENT = 64
BAND = 8
ROWS = 3072
HALF = 512
K1 = 16384
PIECES = 4
PROWS = CENT // PIECES
DP = ("dp_0", "dp_1", "dp_2")
MESH = pl.DeviceIdType.MESH
F32 = jnp.float32
BF16 = jnp.bfloat16


def dot_nt(a, b):
    return lax.dot_general(a, b, (((1,), (1,)), ((), ())), preferred_element_type=F32)


def kernel(
    emb_hbm, ids_ref, sec_ref,
    fc_out, sc_out, scores_out,
    emb, oh, part, csend, crecv, cntpart, cntsend, cntrecv,
    xg, idbuf, oh2, ysend, yrecv, ypart, ycsend, ycrecv, zcsend, zcrecv,
    zsend, zpart, zrecv, zg, bsend, yg, ssend, sret,
    emb_sem, c_ss, c_rs, cc_ss, cc_rs, x_ss, x_rs, id_ss, id_rs, pt_ss, pt_rs,
    y_ss, y_rs, yc_ss, yc_rs, zc_ss, zc_rs, z_ss, z_rs, za_ss, za_rs,
    ya_ss, ya_rs, r_ss, r_rs,
):
    x = lax.axis_index("dp_0")
    y = lax.axis_index("dp_1")
    z = lax.axis_index("dp_2")
    c = lax.axis_index("mp")
    me = (x * NY + y) * NZ + z
    devices = NX * NY * NZ

    def coords(index):
        return (index // (NY * NZ), lax.rem(index // NZ, NY), lax.rem(index, NZ), c)

    after = coords(lax.rem(me + 1, devices))
    before = coords(lax.rem(me + devices - 1, devices))

    def xdev(step, core):
        return (lax.rem(x + step, NX), y, z, core)

    def ydev(step, core):
        return (x, lax.rem(y + step, NY), z, core)

    def zdev(step):
        return (x, y, lax.rem(z + step, NZ), c)

    load = pltpu.make_async_copy(emb_hbm, emb, emb_sem)
    load.start()

    barrier = pltpu.get_barrier_semaphore()
    peers = [after, before, (x, y, z, 1 - c)]
    for step in range(1, NX):
        peers += [xdev(step, 0), xdev(step, 1)]
    for step in range(1, NY):
        peers += [ydev(step, 0), ydev(step, 1)]
    for step in range(1, NZ):
        peers.append(zdev(step))
    for peer in peers:
        pl.semaphore_signal(barrier, inc=1, device_id=peer, device_id_type=MESH)

    pending = []

    def send(src, dst, ssem, rsem, device):
        copy = pltpu.make_async_remote_copy(
            src_ref=src, dst_ref=dst, send_sem=ssem, recv_sem=rsem, device_id=device, device_id_type=MESH
        )
        copy.start()
        pending.append(copy)

    def arrived(dst, ssem, rsem):
        pltpu.make_async_remote_copy(
            src_ref=dst, dst_ref=dst, send_sem=ssem, recv_sem=rsem, device_id=after, device_id_type=MESH
        ).wait_recv()

    shifted = ids_ref[...] - me * CENT
    local = jnp.where(shifted < 0, shifted + K1, shifted)
    ones_row = jnp.ones((8, 128), BF16)

    def one_hot_block(j):
        wanted = lax.broadcasted_iota(jnp.int32, (CENT, ROWS), 0) + j * CENT
        oh[pl.ds(j * CENT, CENT), :] = jnp.where(local == wanted, 1.0, 0.0).astype(BF16)

    def counts_block(j):
        folded = oh[pl.ds(j * CENT, CENT), pl.ds(0, 128)]
        for k in range(1, ROWS // 128):
            folded = folded + oh[pl.ds(j * CENT, CENT), pl.ds(k * 128, 128)]
        cntpart[j, :, pl.ds(0, CENT)] = dot_nt(ones_row, folded)[0:1]

    half = BAND // 2 * CENT
    for j in range(BAND // 2, BAND):
        one_hot_block(j)
    load.wait()
    part[pl.ds(half, half), :] = jnp.dot(oh[pl.ds(half, half), :], emb[...], preferred_element_type=F32)
    cntpart[...] = jnp.zeros_like(cntpart)
    for j in range(BAND // 2, BAND):
        counts_block(j)
    idbuf[x, :, pl.ds(0, CENT)] = sec_ref[...]
    idbuf[x, :, pl.ds(CENT, CENT)] = sec_ref[...]

    pl.semaphore_wait(barrier, len(peers))

    def chain_send(s):
        j = BAND - s
        for p in range(PIECES):
            rows = pl.ds(p * PROWS, PROWS)
            total = part[pl.ds(j * CENT + p * PROWS, PROWS), :]
            if s > 1:
                arrived(crecv.at[s - 2, rows], c_ss.at[s - 2, p], c_rs.at[s - 2, p])
                total = total + crecv[s - 2, rows].astype(F32)
            csend[s - 1, rows] = total.astype(BF16)
            send(csend.at[s - 1, rows], crecv.at[s - 1, rows], c_ss.at[s - 1, p], c_rs.at[s - 1, p], after)
        count = cntpart[j]
        if s > 1:
            arrived(cntrecv.at[s - 2], cc_ss.at[s - 2], cc_rs.at[s - 2])
            count = count + cntrecv[s - 2]
        cntsend[s - 1] = count
        send(cntsend.at[s - 1], cntrecv.at[s - 1], cc_ss.at[s - 1], cc_rs.at[s - 1], after)

    chain_send(1)
    for step in range(1, NX):
        send(idbuf.at[x], idbuf.at[x], id_ss.at[step - 1], id_rs.at[step - 1], xdev(step, c))
    for j in range(BAND // 2):
        one_hot_block(j)
    part[pl.ds(0, half), :] = jnp.dot(oh[pl.ds(0, half), :], emb[...], preferred_element_type=F32)
    for j in range(BAND // 2):
        counts_block(j)
    chain_send(2)

    for step in range(1, NX):
        arrived(idbuf.at[lax.rem(x + NX - step, NX)], id_ss.at[step - 1], id_rs.at[step - 1])
    wide = NY * NZ * 8
    lane = lax.broadcasted_iota(jnp.int32, (1, 128), 1)
    row = lax.broadcasted_iota(jnp.int32, (wide, 128), 0)
    group = x * (NY * NZ * 4) + (row // 8) * 4 + lax.rem(row, 4)
    upper = lax.rem(row, 8) < 4
    for pair in range(NX // 2):
        names = jnp.where(lane < CENT, idbuf[2 * pair], idbuf[2 * pair + 1])
        hit = names == group
        oh2[0, :, pl.ds(pair * 128, 128)] = jnp.where(hit & upper, 1.0, 0.0).astype(BF16)
        oh2[1, :, pl.ds(pair * 128, 128)] = jnp.where(hit & ~upper, 1.0, 0.0).astype(BF16)
    ones_wide = jnp.ones((8, NX * CENT), BF16)
    for k in range(NY):
        rows = pl.ds(k * NZ * 8, NZ * 8)
        ycsend[k] = (dot_nt(ones_wide, oh2[0, rows, :]) + dot_nt(ones_wide, oh2[1, rows, :]))[0:1]
    for step in range(1, NY):
        to = lax.rem(y + step, NY)
        send(ycsend.at[to], ycrecv.at[step - 1], yc_ss.at[step - 1], yc_rs.at[step - 1], ydev(step, c))
    chain_send(3)
    chain_send(4)
    line = ycsend[y]
    for step in range(1, NY):
        arrived(ycrecv.at[step - 1], yc_ss.at[step - 1], yc_rs.at[step - 1])
        line = line + ycrecv[step - 1]
    zcsend[...] = line
    for step in range(1, NZ):
        send(zcsend, zcrecv.at[step - 1], zc_ss.at[step - 1], zc_rs.at[step - 1], zdev(step))
    chain_send(5)
    chain_send(6)
    chain_send(7)

    last = BAND - 2
    arrived(cntrecv.at[last], cc_ss.at[last], cc_rs.at[last])
    count_row = (cntpart[0] + cntrecv[last])[:, 0:CENT]
    eye = lax.broadcasted_iota(jnp.int32, (CENT, CENT), 0) == lax.broadcasted_iota(jnp.int32, (CENT, CENT), 1)
    count_column = jnp.sum(jnp.where(eye, count_row, 0.0), axis=1, keepdims=True)
    for p in range(PIECES):
        rows = pl.ds(p * PROWS, PROWS)
        arrived(crecv.at[last, rows], c_ss.at[last, p], c_rs.at[last, p])
        total = part[rows, :] + crecv[last, rows].astype(F32)
        done = (total / count_column[p * PROWS : (p + 1) * PROWS]).astype(BF16)
        fc_out[rows, :] = done
        xg[c, x, rows] = done
        for step in range(1, NX):
            send(xg.at[c, x, rows], xg.at[c, x, rows], x_ss.at[step - 1, p], x_rs.at[step - 1, p], xdev(step, c))
    for step in range(1, NX):
        source = lax.rem(x + NX - step, NX)
        for p in range(PIECES):
            rows = pl.ds(p * PROWS, PROWS)
            arrived(xg.at[c, source, rows], x_ss.at[step - 1, p], x_rs.at[step - 1, p])
    send(xg.at[c], xg.at[c], pt_ss, pt_rs, (x, y, z, 1 - c))

    mine = xg[c].reshape(NX * CENT, HALF)
    for step in list(range(1, NY)) + [0]:
        to = lax.rem(y + step, NY)
        rows = pl.ds(pl.multiple_of(to * NZ * 8, NZ * 8), NZ * 8)
        sums = jnp.dot(oh2[0, rows, :], mine[:, : HALF // 2], preferred_element_type=F32)
        sums = sums + jnp.dot(oh2[1, rows, :], mine[:, HALF // 2 :], preferred_element_type=F32)
        if step:
            ysend[step - 1] = sums.astype(BF16)
            send(ysend.at[step - 1], yrecv.at[step - 1], y_ss.at[step - 1], y_rs.at[step - 1], ydev(step, c))
        else:
            ypart[...] = sums
    sums = ypart[...]
    for step in range(1, NY):
        arrived(yrecv.at[step - 1], y_ss.at[step - 1], y_rs.at[step - 1])
        sums = sums + yrecv[step - 1].astype(F32)
    zpart[...] = sums.reshape(NZ, 8, HALF // 2)
    zsend[...] = sums.reshape(NZ, 8, HALF // 2).astype(BF16)
    order = sorted(range(1, NZ), key=lambda step: -min(step, NZ - step))
    for step in order:
        to = lax.rem(z + step, NZ)
        send(zsend.at[to], zrecv.at[step - 1], z_ss.at[step - 1], z_rs.at[step - 1], zdev(step))
    counts = zcsend[...]
    for step in range(1, NZ):
        arrived(zcrecv.at[step - 1], zc_ss.at[step - 1], zc_rs.at[step - 1])
        counts = counts + zcrecv[step - 1]
    eight = lax.broadcasted_iota(jnp.int32, (8, 128), 0) + z * 8 == lax.broadcasted_iota(jnp.int32, (8, 128), 1)
    second_counts = jnp.sum(jnp.where(eight, counts, 0.0), axis=1, keepdims=True)
    sums = zpart[z]
    for step in reversed(order):
        arrived(zrecv.at[step - 1], z_ss.at[step - 1], z_rs.at[step - 1])
        sums = sums + zrecv[step - 1].astype(F32)
    second = (sums / second_counts).astype(BF16)
    zg[z] = second
    for step in order:
        send(zg.at[z], zg.at[z], za_ss.at[step - 1], za_rs.at[step - 1], zdev(step))
    second32 = second.astype(F32)
    sc_out[:, pl.ds(0, HALF // 2)] = second32[0:4].astype(BF16)
    sc_out[:, pl.ds(HALF // 2, HALF // 2)] = second32[4:8].astype(BF16)
    for step in reversed(order):
        arrived(zg.at[lax.rem(z + NZ - step, NZ)], za_ss.at[step - 1], za_rs.at[step - 1])

    gathered = zg[...].reshape(NZ * 8, HALF // 2)
    index = lax.broadcasted_iota(jnp.int32, (NZ * 4, NZ * 8), 0)
    column = lax.broadcasted_iota(jnp.int32, (NZ * 4, NZ * 8), 1)
    place = (index // 4) * 8 + lax.rem(index, 4)
    for h in range(2):
        pick = jnp.where(column == place + 4 * h, 1.0, 0.0).astype(BF16)
        picked = jnp.dot(pick, gathered, preferred_element_type=F32).astype(BF16)
        bsend[:, pl.ds(h * (HALF // 2), HALF // 2)] = picked
    scorer = y // (NY // 2)
    slot = lax.rem(y, NY // 2)
    for step in range(1, NY):
        send(bsend, yg.at[c, slot], ya_ss.at[step], ya_rs.at[c, slot], ydev(step, scorer))
    own_scorer = scorer == c

    @pl.when(own_scorer)
    def _():
        yg[c, slot] = bsend[...]

    @pl.when(jnp.logical_not(own_scorer))
    def _():
        pltpu.make_async_remote_copy(
            src_ref=bsend, dst_ref=yg.at[c, slot], send_sem=ya_ss.at[0], recv_sem=ya_rs.at[c, slot],
            device_id=(x, y, z, 1 - c), device_id_type=MESH,
        ).start()

    arrived(xg.at[1 - c], pt_ss, pt_rs)
    for s in range(NY // 2):
        for k in range(2):
            here = jnp.logical_and(c * (NY // 2) + s == y, c == k)

            @pl.when(jnp.logical_not(here))
            def _():
                arrived(yg.at[k, s], ya_ss.at[0], ya_rs.at[k, s])

    groups = NY // 2 * NZ * 4
    scores = jnp.zeros((NX * CENT, groups), F32)
    squares = jnp.zeros((groups, 1), F32)
    for k in range(2):
        b = yg[k].reshape(groups, HALF)
        scores = scores + dot_nt(xg[k].reshape(NX * CENT, HALF), b)
        b32 = b.astype(F32)
        squares = squares + jnp.sum(b32 * b32, axis=1, keepdims=True)
    eye = lax.broadcasted_iota(jnp.int32, (groups, groups), 0) == lax.broadcasted_iota(jnp.int32, (groups, groups), 1)
    norm_row = jnp.sum(jnp.where(eye, squares, 0.0), axis=0, keepdims=True)
    ssend[...] = (scores - 0.5 * norm_row).astype(BF16).reshape(NX, CENT, groups)
    holder = x // (NX // 2)
    out_slot = lax.rem(x, NX // 2) * 2 + c
    for step in range(1, NX):
        to = lax.rem(x + step, NX)
        send(ssend.at[to], sret.at[out_slot], r_ss.at[step], r_rs.at[out_slot], xdev(step, holder))
    own_holder = holder == c

    @pl.when(own_holder)
    def _():
        sret[out_slot] = ssend[x]

    @pl.when(jnp.logical_not(own_holder))
    def _():
        pltpu.make_async_remote_copy(
            src_ref=ssend.at[x], dst_ref=sret.at[out_slot], send_sem=r_ss.at[0], recv_sem=r_rs.at[out_slot],
            device_id=(x, y, z, 1 - c), device_id_type=MESH,
        ).start()

    for s in range(NX):
        here = jnp.logical_and(c * (NX // 2) + s // 2 == x, c == s % 2)

        @pl.when(jnp.logical_not(here))
        def _():
            arrived(sret.at[s], r_ss.at[0], r_rs.at[s])

        scores_out[:, pl.ds(s * groups, groups)] = sret[s].astype(F32)

    for copy in pending:
        copy.wait_send()

    @pl.when(jnp.logical_not(own_scorer))
    def _():
        pltpu.make_async_remote_copy(
            src_ref=bsend, dst_ref=yg.at[c, slot], send_sem=ya_ss.at[0], recv_sem=ya_rs.at[c, slot],
            device_id=(x, y, z, 1 - c), device_id_type=MESH,
        ).wait_send()

    @pl.when(jnp.logical_not(own_holder))
    def _():
        pltpu.make_async_remote_copy(
            src_ref=ssend.at[x], dst_ref=sret.at[out_slot], send_sem=r_ss.at[0], recv_sem=r_rs.at[out_slot],
            device_id=(x, y, z, 1 - c), device_id_type=MESH,
        ).wait_send()


def shards(embeddings, first_level, second_level):
    dma = pltpu.SemaphoreType.DMA
    groups = NY // 2 * NZ * 4
    vmem = pl.BlockSpec(memory_space=pltpu.VMEM)
    return pl.pallas_call(
        kernel,
        out_shape=(
            jax.ShapeDtypeStruct((CENT, HALF), BF16),
            jax.ShapeDtypeStruct((4, HALF), BF16),
            jax.ShapeDtypeStruct((CENT, HALF), F32),
        ),
        in_specs=[pl.BlockSpec(memory_space=pl.ANY), vmem, vmem],
        out_specs=(vmem, vmem, vmem),
        scratch_shapes=[
            pltpu.VMEM((ROWS, HALF), BF16),
            pltpu.VMEM((BAND * CENT, ROWS), BF16),
            pltpu.VMEM((BAND * CENT, HALF), F32),
            pltpu.VMEM((BAND - 1, CENT, HALF), BF16),
            pltpu.VMEM((BAND - 1, CENT, HALF), BF16),
            pltpu.VMEM((BAND, 1, 128), F32),
            pltpu.VMEM((BAND - 1, 1, 128), F32),
            pltpu.VMEM((BAND - 1, 1, 128), F32),
            pltpu.VMEM((2, NX, CENT, HALF), BF16),
            pltpu.VMEM((NX, 1, 128), jnp.int32),
            pltpu.VMEM((2, NY * NZ * 8, NX * CENT), BF16),
            pltpu.VMEM((NY - 1, NZ * 8, HALF // 2), BF16),
            pltpu.VMEM((NY - 1, NZ * 8, HALF // 2), BF16),
            pltpu.VMEM((NZ * 8, HALF // 2), F32),
            pltpu.VMEM((NY, 1, 128), F32),
            pltpu.VMEM((NY - 1, 1, 128), F32),
            pltpu.VMEM((1, 128), F32),
            pltpu.VMEM((NZ - 1, 1, 128), F32),
            pltpu.VMEM((NZ, 8, HALF // 2), BF16),
            pltpu.VMEM((NZ, 8, HALF // 2), F32),
            pltpu.VMEM((NZ - 1, 8, HALF // 2), BF16),
            pltpu.VMEM((NZ, 8, HALF // 2), BF16),
            pltpu.VMEM((NZ * 4, HALF), BF16),
            pltpu.VMEM((2, NY // 2, NZ * 4, HALF), BF16),
            pltpu.VMEM((NX, CENT, groups), BF16),
            pltpu.VMEM((NX, CENT, groups), BF16),
            dma,
            dma((BAND - 1, PIECES)), dma((BAND - 1, PIECES)),
            dma((BAND - 1,)), dma((BAND - 1,)),
            dma((NX - 1, PIECES)), dma((NX - 1, PIECES)),
            dma((NX - 1,)), dma((NX - 1,)),
            dma, dma,
            dma((NY - 1,)), dma((NY - 1,)),
            dma((NY - 1,)), dma((NY - 1,)),
            dma((NZ - 1,)), dma((NZ - 1,)),
            dma((NZ - 1,)), dma((NZ - 1,)),
            dma((NZ - 1,)), dma((NZ - 1,)),
            dma((NY,)), dma((2, NY // 2)),
            dma((NX,)), dma((NX,)),
        ],
        compiler_params=pltpu.CompilerParams(
            collective_id=0, has_side_effects=True, vmem_limit_bytes=48 << 20
        ),
        name="update",
    )(embeddings, first_level.reshape(1, ROWS), second_level.reshape(1, CENT))


def solution(mesh):
    torus = Mesh(mesh.devices.reshape(NX, NY, NZ, mesh.shape["mp"]), (*DP, "mp"))
    return jax.shard_map(
        shards,
        mesh=torus,
        in_specs=(P(DP, "mp"), P(DP), P(DP, None)),
        out_specs=(P(DP, "mp"), P(DP, "mp"), P(DP, "mp")),
        check_vma=False,
    )
```

```python
import jax
import jax.numpy as jnp
from jax import lax
from jax.experimental import pallas as pl
from jax.experimental.pallas import tpu as pltpu
from jax.sharding import Mesh
from jax.sharding import PartitionSpec as P

NX, NY, NZ = 4, 4, 16
CENT = 64
BAND = 8
ROWS = 3072
HALF = 512
K1 = 16384
PIECES = 2
PROWS = CENT // PIECES
DP = ("dp_0", "dp_1", "dp_2")
MESH = pl.DeviceIdType.MESH
F32 = jnp.float32
BF16 = jnp.bfloat16


def dot_nt(a, b):
    return lax.dot_general(a, b, (((1,), (1,)), ((), ())), preferred_element_type=F32)


def kernel(
    emb_hbm, ids_hbm, sec_hbm,
    fc_out, sc_out, sret,
    ids_ref, sec_ref, emb, oh, part, csend, crecv, table, tables, xg, idbuf,
    asend, arecv, apart, bsend, brecv, bpart, a2send, a2recv, b2send, b2recv,
    ycsend, ycrecv, zcsend, zcrecv, zsend, zpart, zrecv, zg, gsend, yg, ssend,
    emb_sem, ids_sem, sec_sem, t_ss, t_rs, c_ss, c_rs, x_ss, x_rs, id_ss, id_rs, pt_ss, pt_rs,
    a_ss, a_rs, b_ss, b_rs, a2_ss, a2_rs, b2_ss, b2_rs,
    yc_ss, yc_rs, zc_ss, zc_rs, z_ss, z_rs, za_ss, za_rs, ya_ss, ya_rs, r_ss, r_rs,
):
    x = lax.axis_index("dp_0")
    y = lax.axis_index("dp_1")
    z = lax.axis_index("dp_2")
    c = lax.axis_index("mp")
    me = (x * NY + y) * NZ + z
    devices = NX * NY * NZ

    def chip(step):
        index = lax.rem(me + step + devices, devices)
        return (index // (NY * NZ), lax.rem(index // NZ, NY), lax.rem(index, NZ), c)

    def xdev(step, core):
        return (lax.rem(x + step, NX), y, z, core)

    def ydev(step, core):
        return (x, lax.rem(y + step, NY), z, core)

    def zdev(step):
        return (x, y, lax.rem(z + step, NZ), c)

    partner = (x, y, z, 1 - c)
    load_ids = pltpu.make_async_copy(ids_hbm, ids_ref, ids_sem)
    load_sec = pltpu.make_async_copy(sec_hbm, sec_ref, sec_sem)
    load = pltpu.make_async_copy(emb_hbm, emb, emb_sem)
    load_ids.start()
    load_sec.start()
    load.start()

    barrier = pltpu.get_barrier_semaphore()
    near = [d for k in range(1, BAND) for d in (k, -k)]
    peers = [partner] + [chip(d) for d in near]
    for step in range(1, NX):
        peers += [xdev(step, 0), xdev(step, 1)]
    for step in range(1, NY):
        peers += [ydev(step, 0), ydev(step, 1)]
    for step in range(1, NZ):
        peers.append(zdev(step))
    for peer in peers:
        pl.semaphore_signal(barrier, inc=1, device_id=peer, device_id_type=MESH)

    pending = []

    def send(src, dst, ssem, rsem, device):
        copy = pltpu.make_async_remote_copy(
            src_ref=src, dst_ref=dst, send_sem=ssem, recv_sem=rsem, device_id=device, device_id_type=MESH
        )
        copy.start()
        pending.append(copy)

    def arrived(dst, ssem, rsem):
        pltpu.make_async_remote_copy(
            src_ref=dst, dst_ref=dst, send_sem=ssem, recv_sem=rsem, device_id=partner, device_id_type=MESH
        ).wait_recv()

    load_ids.wait()
    shifted = ids_ref[...] - me * CENT
    local = jnp.where(shifted < 0, shifted + K1, shifted)
    ones_row = jnp.ones((8, 128), BF16)
    load_sec.wait()
    table[...] = jnp.zeros_like(table)
    table[0, :, pl.ds(CENT, CENT)] = sec_ref[...].astype(F32)
    idbuf[x, :, pl.ds(0, CENT)] = sec_ref[...]
    idbuf[x, :, pl.ds(CENT, CENT)] = sec_ref[...]
    for j in range(BAND):
        rows = pl.ds(j * CENT, CENT)
        wanted = lax.broadcasted_iota(jnp.int32, (CENT, ROWS), 0) + j * CENT
        oh[rows, :] = jnp.where(local == wanted, 1.0, 0.0).astype(BF16)
        folded = oh[rows, pl.ds(0, 128)]
        for k in range(1, ROWS // 128):
            folded = folded + oh[rows, pl.ds(k * 128, 128)]
        table[j, :, pl.ds(0, CENT)] = dot_nt(ones_row, folded)[0:1]

    pl.semaphore_wait(barrier, len(peers))

    for d in near:
        kept = pl.ds(d, BAND - d) if d > 0 else pl.ds(0, BAND + d)
        t = d + BAND - 1
        send(table.at[kept], tables.at[t, kept], t_ss.at[t], t_rs.at[t], chip(d))
    for step in range(1, NX):
        send(idbuf.at[x], idbuf.at[x], id_ss.at[step - 1], id_rs.at[step - 1], xdev(step, c))

    def chain_send(s):
        j = BAND - s
        for p in range(PIECES):
            rows = pl.ds(p * PROWS, PROWS)
            total = part[pl.ds(j * CENT + p * PROWS, PROWS), :]
            if s > 1:
                arrived(crecv.at[s - 2, rows], c_ss.at[s - 2, p], c_rs.at[s - 2, p])
                total = total + crecv[s - 2, rows].astype(F32)
            csend[s - 1, rows] = total.astype(BF16)
            send(csend.at[s - 1, rows], crecv.at[s - 1, rows], c_ss.at[s - 1, p], c_rs.at[s - 1, p], chip(1))

    half = BAND // 2 * CENT
    load.wait()
    part[pl.ds(half, half), :] = jnp.dot(oh[pl.ds(half, half), :], emb[...], preferred_element_type=F32)
    chain_send(1)
    part[pl.ds(0, half), :] = jnp.dot(oh[pl.ds(0, half), :], emb[...], preferred_element_type=F32)

    for step in range(1, NX):
        arrived(idbuf.at[lax.rem(x + NX - step, NX)], id_ss.at[step - 1], id_rs.at[step - 1])
    lane = lax.broadcasted_iota(jnp.int32, (1, 128), 1)
    row = lax.broadcasted_iota(jnp.int32, (NY * NZ * 8, 128), 0)
    group = x * (NY * NZ * 4) + (row // 8) * 4 + lax.rem(row, 4)
    hits = []
    for pair in range(NX // 2):
        names = jnp.where(lane < CENT, idbuf[2 * pair], idbuf[2 * pair + 1])
        hits.append(jnp.where(names == group, 1.0, 0.0))
    hit = (hits[0] + hits[1]).astype(BF16)
    for k in range(NY):
        ycsend[k] = dot_nt(ones_row, hit[k * NZ * 8 : (k + 1) * NZ * 8])[0:1]
    for step in range(1, NY):
        to = lax.rem(y + step, NY)
        send(ycsend.at[to], ycrecv.at[step - 1], yc_ss.at[step - 1], yc_rs.at[step - 1], ydev(step, c))
    chain_send(2)

    for d in near:
        kept = pl.ds(d, BAND - d) if d > 0 else pl.ds(0, BAND + d)
        t = d + BAND - 1
        arrived(tables.at[t, kept], t_ss.at[t], t_rs.at[t])
    eye = lax.broadcasted_iota(jnp.int32, (CENT, CENT), 0) == lax.broadcasted_iota(jnp.int32, (CENT, CENT), 1)
    columns, name_rows = [], []
    for j in range(BAND):
        total = table[j]
        for d in near:
            k = j + d
            if 0 <= k < BAND:
                total = total + tables[d + BAND - 1, k]
        columns.append(jnp.sum(jnp.where(eye, total[:, 0:CENT], 0.0), axis=1, keepdims=True))
        name_rows.append(table[0] if j == 0 else tables[BAND - 1 - j, 0])
    names = jnp.concatenate(
        [
            jnp.where(lane < CENT, pltpu.roll(name_rows[2 * k], CENT, 1), name_rows[2 * k + 1])
            for k in range(BAND // 2)
        ],
        axis=1,
    ).astype(jnp.int32)
    scaled = jnp.concatenate(
        [(part[pl.ds(j * CENT, CENT), :] / columns[j]).astype(BF16) for j in range(BAND)], axis=0
    )

    block = NY * NZ * 4
    quarter = NZ * 4
    fold = HALF // 2
    for step in list(range(1, NX)) + [0]:
        to = lax.rem(x + step, NX)
        wanted = lax.broadcasted_iota(jnp.int32, (block, BAND * CENT), 0) + to * block
        member = jnp.where(names == wanted, 1.0, 0.0).astype(BF16)
        sums = jnp.dot(member, scaled, preferred_element_type=F32)
        if step:
            asend[step - 1] = sums[:, :fold].astype(BF16)
            send(asend.at[step - 1], arecv.at[step - 1], a_ss.at[step - 1], a_rs.at[step - 1], xdev(step, c))
        else:
            apart[...] = sums[:, :fold]
        for k in range(NY):
            piece = sums[k * quarter : (k + 1) * quarter, fold:]
            bsend[k, to] = piece.astype(BF16)
            bpart[k, to] = piece
    for step in range(1, NY):
        to = lax.rem(y + step, NY)
        send(bsend.at[to], brecv.at[step - 1], b_ss.at[step - 1], b_rs.at[step - 1], ydev(step, c))
    chain_send(3)
    line = ycsend[y]
    for step in range(1, NY):
        arrived(ycrecv.at[step - 1], yc_ss.at[step - 1], yc_rs.at[step - 1])
        line = line + ycrecv[step - 1]
    zcsend[...] = line
    order = sorted(range(1, NZ), key=lambda step: -min(step, NZ - step))
    for step in order:
        send(zcsend, zcrecv.at[step - 1], zc_ss.at[step - 1], zc_rs.at[step - 1], zdev(step))
    chain_send(4)

    for step in range(1, NX):
        arrived(arecv.at[step - 1], a_ss.at[step - 1], a_rs.at[step - 1])
    for step in list(range(1, NY)) + [0]:
        to = lax.rem(y + step, NY)
        rows = pl.ds(pl.multiple_of(to * quarter, quarter), quarter)
        sums = apart[rows, :]
        for k in range(NX - 1):
            sums = sums + arecv[k, rows].astype(F32)
        if step:
            a2send[step - 1] = sums.astype(BF16)
            send(a2send.at[step - 1], a2recv.at[step - 1], a2_ss.at[step - 1], a2_rs.at[step - 1], ydev(step, c))
    first_half = sums
    for step in range(1, NY):
        arrived(brecv.at[step - 1], b_ss.at[step - 1], b_rs.at[step - 1])
    for step in list(range(1, NX)) + [0]:
        to = lax.rem(x + step, NX)
        sums = bpart[y, to]
        for k in range(NY - 1):
            sums = sums + brecv[k, to].astype(F32)
        if step:
            b2send[step - 1] = sums.astype(BF16)
            send(b2send.at[step - 1], b2recv.at[step - 1], b2_ss.at[step - 1], b2_rs.at[step - 1], xdev(step, c))
    second_half = sums
    chain_send(5)
    for step in range(1, NY):
        arrived(a2recv.at[step - 1], a2_ss.at[step - 1], a2_rs.at[step - 1])
        first_half = first_half + a2recv[step - 1].astype(F32)
    for step in range(1, NX):
        arrived(b2recv.at[step - 1], b2_ss.at[step - 1], b2_rs.at[step - 1])
        second_half = second_half + b2recv[step - 1].astype(F32)

    first_half = first_half.reshape(NZ // 2, 8, fold)
    second_half = second_half.reshape(NZ // 2, 8, fold)
    low = lax.broadcasted_iota(jnp.int32, (NZ // 2, 8, fold), 1) < 4
    even = jnp.where(low, first_half, pltpu.roll(second_half, 4, 1))
    odd = jnp.where(low, pltpu.roll(first_half, 4, 1), second_half)
    for k in range(NZ // 2):
        zpart[2 * k] = even[k]
        zpart[2 * k + 1] = odd[k]
    zsend[...] = zpart[...].astype(BF16)
    for step in order:
        to = lax.rem(z + step, NZ)
        send(zsend.at[to], zrecv.at[step - 1], z_ss.at[step - 1], z_rs.at[step - 1], zdev(step))
    chain_send(6)
    counts = zcsend[...]
    for step in range(1, NZ):
        arrived(zcrecv.at[step - 1], zc_ss.at[step - 1], zc_rs.at[step - 1])
        counts = counts + zcrecv[step - 1]
    eight = lax.broadcasted_iota(jnp.int32, (8, 128), 0) + z * 8 == lax.broadcasted_iota(jnp.int32, (8, 128), 1)
    second_counts = jnp.sum(jnp.where(eight, counts, 0.0), axis=1, keepdims=True)
    sums = zpart[z]
    for step in reversed(order):
        arrived(zrecv.at[step - 1], z_ss.at[step - 1], z_rs.at[step - 1])
        sums = sums + zrecv[step - 1].astype(F32)
    second = (sums / second_counts).astype(BF16)
    zg[z] = second
    for step in order:
        send(zg.at[z], zg.at[z], za_ss.at[step - 1], za_rs.at[step - 1], zdev(step))
    second32 = second.astype(F32)
    sc_out[:, pl.ds(0, fold)] = second32[0:4].astype(BF16)
    sc_out[:, pl.ds(fold, fold)] = second32[4:8].astype(BF16)
    chain_send(7)

    last = BAND - 2
    for p in range(PIECES):
        rows = pl.ds(p * PROWS, PROWS)
        arrived(crecv.at[last, rows], c_ss.at[last, p], c_rs.at[last, p])
        total = part[rows, :] + crecv[last, rows].astype(F32)
        done = (total / columns[0][p * PROWS : (p + 1) * PROWS]).astype(BF16)
        fc_out[rows, :] = done
        xg[c, x, rows] = done
        for step in range(1, NX):
            send(xg.at[c, x, rows], xg.at[c, x, rows], x_ss.at[step - 1, p], x_rs.at[step - 1, p], xdev(step, c))
    for step in range(1, NX):
        source = lax.rem(x + NX - step, NX)
        for p in range(PIECES):
            rows = pl.ds(p * PROWS, PROWS)
            arrived(xg.at[c, source, rows], x_ss.at[step - 1, p], x_rs.at[step - 1, p])
    send(xg.at[c], xg.at[c], pt_ss, pt_rs, partner)
    for step in reversed(order):
        arrived(zg.at[lax.rem(z + NZ - step, NZ)], za_ss.at[step - 1], za_rs.at[step - 1])

    gathered = zg[...].reshape(NZ * 8, fold)
    index = lax.broadcasted_iota(jnp.int32, (quarter, NZ * 8), 0)
    column = lax.broadcasted_iota(jnp.int32, (quarter, NZ * 8), 1)
    place = (index // 4) * 8 + lax.rem(index, 4)
    for h in range(2):
        pick = jnp.where(column == place + 4 * h, 1.0, 0.0).astype(BF16)
        picked = jnp.dot(pick, gathered, preferred_element_type=F32).astype(BF16)
        gsend[:, pl.ds(h * fold, fold)] = picked
    scorer = y // (NY // 2)
    slot = lax.rem(y, NY // 2)
    for step in range(1, NY):
        send(gsend, yg.at[c, slot], ya_ss.at[step], ya_rs.at[c, slot], ydev(step, scorer))
    own_scorer = scorer == c
    to_scorer = pltpu.make_async_remote_copy(
        src_ref=gsend, dst_ref=yg.at[c, slot], send_sem=ya_ss.at[0], recv_sem=ya_rs.at[c, slot],
        device_id=partner, device_id_type=MESH,
    )

    @pl.when(own_scorer)
    def _():
        yg[c, slot] = gsend[...]

    @pl.when(jnp.logical_not(own_scorer))
    def _():
        to_scorer.start()

    arrived(xg.at[1 - c], pt_ss, pt_rs)
    for s in range(NY // 2):
        for k in range(2):
            here = jnp.logical_and(c * (NY // 2) + s == y, c == k)

            @pl.when(jnp.logical_not(here))
            def _():
                arrived(yg.at[k, s], ya_ss.at[0], ya_rs.at[k, s])

    groups = NY // 2 * quarter
    scores = jnp.zeros((NX * CENT, groups), F32)
    squares = jnp.zeros((groups, 1), F32)
    for k in range(2):
        b = yg[k].reshape(groups, HALF)
        scores = scores + dot_nt(xg[k].reshape(NX * CENT, HALF), b)
        b32 = b.astype(F32)
        squares = squares + jnp.sum(b32 * b32, axis=1, keepdims=True)
    eye = lax.broadcasted_iota(jnp.int32, (groups, groups), 0) == lax.broadcasted_iota(jnp.int32, (groups, groups), 1)
    norm_row = jnp.sum(jnp.where(eye, squares, 0.0), axis=0, keepdims=True)
    ssend[...] = (scores - 0.5 * norm_row).astype(BF16).reshape(NX, CENT, groups)
    holder = x // (NX // 2)
    out_slot = lax.rem(x, NX // 2) * 2 + c
    for step in range(1, NX):
        to = lax.rem(x + step, NX)
        send(ssend.at[to], sret.at[out_slot], r_ss.at[step], r_rs.at[out_slot], xdev(step, holder))
    own_holder = holder == c
    to_holder = pltpu.make_async_remote_copy(
        src_ref=ssend.at[x], dst_ref=sret.at[out_slot], send_sem=r_ss.at[0], recv_sem=r_rs.at[out_slot],
        device_id=partner, device_id_type=MESH,
    )

    @pl.when(own_holder)
    def _():
        sret[out_slot] = ssend[x]

    @pl.when(jnp.logical_not(own_holder))
    def _():
        to_holder.start()

    for copy in pending:
        copy.wait_send()

    @pl.when(jnp.logical_not(own_scorer))
    def _():
        to_scorer.wait_send()

    @pl.when(jnp.logical_not(own_holder))
    def _():
        to_holder.wait_send()

    for s in range(NX):
        here = jnp.logical_and(c * (NX // 2) + s // 2 == x, c == s % 2)

        @pl.when(jnp.logical_not(here))
        def _():
            arrived(sret.at[s], r_ss.at[0], r_rs.at[s])


def write_out(fc, sc, sret, fc_out, sc_out, scores_out, wide, sems):
    copies = [
        pltpu.make_async_copy(fc, fc_out, sems.at[0]),
        pltpu.make_async_copy(sc, sc_out, sems.at[1]),
    ]
    for copy in copies:
        copy.start()
    groups = sret.shape[2]
    for s in range(NX):
        wide[:, pl.ds(s * groups, groups)] = sret[s].astype(F32)
    copies.append(pltpu.make_async_copy(wide, scores_out, sems.at[2]))
    copies[2].start()
    for copy in copies:
        copy.wait()


def shards(embeddings, first_level, second_level):
    dma = pltpu.SemaphoreType.DMA
    block = NY * NZ * 4
    quarter = NZ * 4
    groups = NY // 2 * quarter
    fold = HALF // 2
    vmem = pl.BlockSpec(memory_space=pltpu.VMEM)
    hbm = pl.BlockSpec(memory_space=pltpu.HBM)
    operands = (embeddings, first_level.reshape(1, ROWS), second_level.reshape(1, CENT))
    first, second, returned = pl.pallas_call(
        kernel,
        out_shape=(
            jax.ShapeDtypeStruct((CENT, HALF), BF16),
            jax.ShapeDtypeStruct((4, HALF), BF16),
            jax.ShapeDtypeStruct((NX, CENT, groups), BF16),
        ),
        in_specs=[hbm] * 3,
        out_specs=(vmem,) * 3,
        scratch_shapes=[
            pltpu.VMEM((1, ROWS), jnp.int32),
            pltpu.VMEM((1, CENT), jnp.int32),
            pltpu.VMEM((ROWS, HALF), BF16),
            pltpu.VMEM((BAND * CENT, ROWS), BF16),
            pltpu.VMEM((BAND * CENT, HALF), F32),
            pltpu.VMEM((BAND - 1, CENT, HALF), BF16),
            pltpu.VMEM((BAND - 1, CENT, HALF), BF16),
            pltpu.VMEM((BAND, 1, 128), F32),
            pltpu.VMEM((2 * BAND - 1, BAND, 1, 128), F32),
            pltpu.VMEM((2, NX, CENT, HALF), BF16),
            pltpu.VMEM((NX, 1, 128), jnp.int32),
            pltpu.VMEM((NX - 1, block, fold), BF16),
            pltpu.VMEM((NX - 1, block, fold), BF16),
            pltpu.VMEM((block, fold), F32),
            pltpu.VMEM((NY, NX, quarter, fold), BF16),
            pltpu.VMEM((NY - 1, NX, quarter, fold), BF16),
            pltpu.VMEM((NY, NX, quarter, fold), F32),
            pltpu.VMEM((NY - 1, quarter, fold), BF16),
            pltpu.VMEM((NY - 1, quarter, fold), BF16),
            pltpu.VMEM((NX - 1, quarter, fold), BF16),
            pltpu.VMEM((NX - 1, quarter, fold), BF16),
            pltpu.VMEM((NY, 1, 128), F32),
            pltpu.VMEM((NY - 1, 1, 128), F32),
            pltpu.VMEM((1, 128), F32),
            pltpu.VMEM((NZ - 1, 1, 128), F32),
            pltpu.VMEM((NZ, 8, fold), BF16),
            pltpu.VMEM((NZ, 8, fold), F32),
            pltpu.VMEM((NZ - 1, 8, fold), BF16),
            pltpu.VMEM((NZ, 8, fold), BF16),
            pltpu.VMEM((quarter, HALF), BF16),
            pltpu.VMEM((2, NY // 2, quarter, HALF), BF16),
            pltpu.VMEM((NX, CENT, groups), BF16),
            dma, dma, dma,
            dma((2 * BAND - 1,)), dma((2 * BAND - 1,)),
            dma((BAND - 1, PIECES)), dma((BAND - 1, PIECES)),
            dma((NX - 1, PIECES)), dma((NX - 1, PIECES)),
            dma((NX - 1,)), dma((NX - 1,)),
            dma, dma,
            dma((NX - 1,)), dma((NX - 1,)),
            dma((NY - 1,)), dma((NY - 1,)),
            dma((NY - 1,)), dma((NY - 1,)),
            dma((NX - 1,)), dma((NX - 1,)),
            dma((NY - 1,)), dma((NY - 1,)),
            dma((NZ - 1,)), dma((NZ - 1,)),
            dma((NZ - 1,)), dma((NZ - 1,)),
            dma((NZ - 1,)), dma((NZ - 1,)),
            dma((NY,)), dma((2, NY // 2)),
            dma((NX,)), dma((NX,)),
        ],
        compiler_params=pltpu.CompilerParams(
            collective_id=0, has_side_effects=True, vmem_limit_bytes=40 << 20
        ),
        name="update",
    )(*(pltpu.with_memory_space_constraint(a, pltpu.HBM) for a in operands))
    return pl.pallas_call(
        write_out,
        out_shape=(
            jax.ShapeDtypeStruct((CENT, HALF), BF16),
            jax.ShapeDtypeStruct((4, HALF), BF16),
            jax.ShapeDtypeStruct((CENT, HALF), F32),
        ),
        in_specs=[vmem] * 3,
        out_specs=(hbm,) * 3,
        scratch_shapes=[pltpu.VMEM((CENT, HALF), F32), dma((3,))],
        compiler_params=pltpu.CompilerParams(vmem_limit_bytes=8 << 20),
        name="write_out",
    )(first, second, returned)


def solution(mesh):
    torus = Mesh(mesh.devices.reshape(NX, NY, NZ, mesh.shape["mp"]), (*DP, "mp"))
    return jax.shard_map(
        shards,
        mesh=torus,
        in_specs=(P(DP, "mp"), P(DP), P(DP, None)),
        out_specs=(P(DP, "mp"), P(DP, "mp"), P(DP, "mp")),
        check_vma=False,
    )
```

```python
import jax
import jax.numpy as jnp
from jax import lax
from jax.experimental import pallas as pl
from jax.experimental.pallas import tpu as pltpu
from jax.sharding import Mesh
from jax.sharding import PartitionSpec as P

NX, NY, NZ = 4, 4, 16
CENT = 64
BAND = 8
ROWS = 3072
HALF = 512
K1 = 16384
DP = ("dp_0", "dp_1", "dp_2")
MESH = pl.DeviceIdType.MESH
F32 = jnp.float32
BF16 = jnp.bfloat16


def dot_nt(a, b):
    return lax.dot_general(a, b, (((1,), (1,)), ((), ())), preferred_element_type=F32)


def kernel(
    emb_hbm, ids_hbm, sec_hbm,
    fc_out, sc_out, sret,
    ids_ref, sec_ref, emb, oh, part, partb, csend, crecv, table, tables, xg, idbuf,
    asend, arecv, apart, bsend, brecv, bpart, a2send, a2recv, b2send, b2recv,
    ycsend, ycrecv, zcsend, zcrecv, zsend, zpart, zrecv, zg, yg, ssend,
    emb_sem, ids_sem, sec_sem, t_ss, t_rs, c_ss, c_rs, x_ss, x_rs, id_ss, id_rs, pt_ss, pt_rs,
    a_ss, a_rs, b_ss, b_rs, a2_ss, a2_rs, b2_ss, b2_rs,
    yc_ss, yc_rs, zc_ss, zc_rs, z_ss, z_rs, za_ss, za_rs, ya_ss, ya_rs, pg_ss, r_ss, r_rs,
):
    x = lax.axis_index("dp_0")
    y = lax.axis_index("dp_1")
    z = lax.axis_index("dp_2")
    c = lax.axis_index("mp")
    me = (x * NY + y) * NZ + z
    devices = NX * NY * NZ

    def chip(step):
        index = lax.rem(me + step + devices, devices)
        return (index // (NY * NZ), lax.rem(index // NZ, NY), lax.rem(index, NZ), c)

    def xdev(step, core):
        return (lax.rem(x + step, NX), y, z, core)

    def ydev(step, core):
        return (x, lax.rem(y + step, NY), z, core)

    def zdev(step):
        return (x, y, lax.rem(z + step, NZ), c)

    partner = (x, y, z, 1 - c)
    load_ids = pltpu.make_async_copy(ids_hbm, ids_ref, ids_sem)
    load_sec = pltpu.make_async_copy(sec_hbm, sec_ref, sec_sem)
    load = pltpu.make_async_copy(emb_hbm, emb, emb_sem)
    load_ids.start()
    load_sec.start()
    load.start()

    barrier = pltpu.get_barrier_semaphore()
    near = [d for k in range(1, BAND) for d in (k, -k)]
    peers = [partner] + [chip(d) for d in near]
    for step in range(1, NX):
        peers += [xdev(step, 0), xdev(step, 1)]
    for step in range(1, NY):
        peers += [ydev(step, 0), ydev(step, 1)]
    for step in range(1, NZ):
        peers.append(zdev(step))
    for peer in peers:
        pl.semaphore_signal(barrier, inc=1, device_id=peer, device_id_type=MESH)

    pending = []

    def send(src, dst, ssem, rsem, device):
        copy = pltpu.make_async_remote_copy(
            src_ref=src, dst_ref=dst, send_sem=ssem, recv_sem=rsem, device_id=device, device_id_type=MESH
        )
        copy.start()
        pending.append(copy)

    def drain():
        while pending:
            pending.pop(0).wait_send()

    def arrived(dst, ssem, rsem):
        pltpu.make_async_remote_copy(
            src_ref=dst, dst_ref=dst, send_sem=ssem, recv_sem=rsem, device_id=partner, device_id_type=MESH
        ).wait_recv()

    load_ids.wait()
    shifted = ids_ref[...] - me * CENT
    local = jnp.where(shifted < 0, shifted + K1, shifted)
    ones_row = jnp.ones((8, 128), BF16)
    load_sec.wait()
    table[...] = jnp.zeros_like(table)
    table[0, :, pl.ds(CENT, CENT)] = sec_ref[...].astype(F32)
    idbuf[x, :, pl.ds(0, CENT)] = sec_ref[...]
    idbuf[x, :, pl.ds(CENT, CENT)] = sec_ref[...]
    for j in range(BAND):
        rows = pl.ds(j * CENT, CENT)
        wanted = lax.broadcasted_iota(jnp.int32, (CENT, ROWS), 0) + j * CENT
        oh[rows, :] = jnp.where(local == wanted, 1.0, 0.0).astype(BF16)
        folded = oh[rows, pl.ds(0, 128)]
        for k in range(1, ROWS // 128):
            folded = folded + oh[rows, pl.ds(k * 128, 128)]
        table[j, :, pl.ds(0, CENT)] = dot_nt(ones_row, folded)[0:1]

    pl.semaphore_wait(barrier, len(peers))

    for d in near:
        kept = pl.ds(d, BAND - d) if d > 0 else pl.ds(0, BAND + d)
        t = d + BAND - 1
        send(table.at[kept], tables.at[t, kept], t_ss.at[t], t_rs.at[t], chip(d))
    for step in range(1, NX):
        send(idbuf.at[x], idbuf.at[x], id_ss.at[step - 1], id_rs.at[step - 1], xdev(step, c))

    def band(j):
        return pl.ds(j * CENT, CENT)

    def step_one(q):
        send(partb.at[band(2 * q + 1)], crecv.at[q], c_ss.at[q], c_rs.at[q], chip(1))

    def joined(j):
        arrived(crecv.at[j // 2], c_ss.at[j // 2], c_rs.at[j // 2])
        return part[band(j), :] + crecv[j // 2].astype(F32)

    def step_two(j):
        k = 4 + j // 4
        csend[k - 4] = joined(j).astype(BF16)
        send(csend.at[k - 4], crecv.at[k], c_ss.at[k], c_rs.at[k], chip(2))

    def received(k):
        arrived(crecv.at[k], c_ss.at[k], c_rs.at[k])
        return crecv[k].astype(F32)

    def step_three():
        csend[2] = (joined(4) + received(5)).astype(BF16)
        send(csend.at[2], crecv.at[6], c_ss.at[6], c_rs.at[6], chip(4))

    half = BAND // 2 * CENT
    load.wait()
    for begin in (half, 0):
        rows = pl.ds(begin, half)
        sums = jnp.dot(oh[rows, :], emb[...], preferred_element_type=F32)
        part[rows, :] = sums
        partb[rows, :] = sums.astype(BF16)
        if begin:
            step_one(3)
            step_one(2)

    step_one(1)
    step_one(0)
    for step in range(1, NX):
        arrived(idbuf.at[lax.rem(x + NX - step, NX)], id_ss.at[step - 1], id_rs.at[step - 1])
    lane = lax.broadcasted_iota(jnp.int32, (1, 128), 1)
    block = NY * NZ * 4
    quarter = NZ * 4
    group = lax.broadcasted_iota(jnp.int32, (block, 128), 0) + x * block
    hits = []
    for pair in range(NX // 2):
        names = jnp.where(lane < CENT, idbuf[2 * pair], idbuf[2 * pair + 1])
        hits.append(jnp.where(names == group, 1.0, 0.0))
    hit = (hits[0] + hits[1]).astype(BF16)
    ycsend[...] = jnp.zeros_like(ycsend)
    for k in range(NY):
        ycsend[k, :, pl.ds(0, CENT)] = dot_nt(ones_row, hit[k * quarter : (k + 1) * quarter])[0:1]
    for step in range(1, NY):
        to = lax.rem(y + step, NY)
        send(ycsend.at[to], ycrecv.at[step - 1], yc_ss.at[step - 1], yc_rs.at[step - 1], ydev(step, c))
    step_two(6)

    for d in near:
        kept = pl.ds(d, BAND - d) if d > 0 else pl.ds(0, BAND + d)
        t = d + BAND - 1
        arrived(tables.at[t, kept], t_ss.at[t], t_rs.at[t])
    totals, name_rows = [], []
    for j in range(BAND):
        total = table[j]
        for d in near:
            k = j + d
            if 0 <= k < BAND:
                total = total + tables[d + BAND - 1, k]
        totals.append(total)
        name_rows.append(table[0] if j == 0 else tables[BAND - 1 - j, 0])
    names, weights = [], []
    for k in range(BAND // 2):
        names.append(jnp.where(lane < CENT, pltpu.roll(name_rows[2 * k], CENT, 1), name_rows[2 * k + 1]))
        weights.append(1.0 / jnp.where(lane < CENT, totals[2 * k], pltpu.roll(totals[2 * k + 1], CENT, 1)))
    names = jnp.concatenate(names, axis=1).astype(jnp.int32)
    weights = jnp.concatenate(weights, axis=1)

    fold = HALF // 2
    far_x = [2, 1, 3, 0]
    far_y = [2, 1, 3, 0]
    for step in far_x:
        to = lax.rem(x + step, NX)
        wanted = lax.broadcasted_iota(jnp.int32, (block, BAND * CENT), 0) + to * block
        member = jnp.where(names == wanted, weights, 0.0).astype(BF16)
        sums = jnp.dot(member, partb[...], preferred_element_type=F32)
        for k in range(NY):
            apart[step, k] = sums[k * quarter : (k + 1) * quarter, :fold]
            bpart[k, to] = sums[k * quarter : (k + 1) * quarter, fold:]
        if step:
            asend[step - 1] = sums[:, :fold].reshape(NY, quarter, fold).astype(BF16)
        for k in far_y:
            at = lax.rem(y + k, NY)
            if step:
                send(
                    asend.at[step - 1, at], arecv.at[step - 1, at],
                    a_ss.at[step - 1, k], a_rs.at[step - 1, k], xdev(step, c),
                )
            if k:
                bsend[k - 1, step] = bpart[at, to].astype(BF16)
                send(
                    bsend.at[k - 1, step], brecv.at[k - 1, to],
                    b_ss.at[k - 1, step], b_rs.at[k - 1, to], ydev(k, c),
                )
    step_two(2)
    step_three()
    line = ycsend[y]
    for step in range(1, NY):
        arrived(ycrecv.at[step - 1], yc_ss.at[step - 1], yc_rs.at[step - 1])
        line = line + ycrecv[step - 1]
    zcsend[...] = line
    order = sorted(range(1, NZ), key=lambda step: -min(step, NZ - step))
    for step in order:
        send(zcsend, zcrecv.at[step - 1], zc_ss.at[step - 1], zc_rs.at[step - 1], zdev(step))

    for t in range(NY):
        step = far_y[t]
        to = lax.rem(y + step, NY)
        sums = apart[0, to]
        for k in range(1, NX):
            arrived(arecv.at[k - 1, to], a_ss.at[k - 1, step], a_rs.at[k - 1, step])
            sums = sums + arecv[k - 1, to].astype(F32)
        if step:
            a2send[step - 1] = sums.astype(BF16)
            send(a2send.at[step - 1], a2recv.at[step - 1], a2_ss.at[step - 1], a2_rs.at[step - 1], ydev(step, c))
        else:
            first_half = sums
        step = far_x[t]
        to = lax.rem(x + step, NX)
        sums = bpart[y, to]
        for k in range(1, NY):
            arrived(brecv.at[k - 1, to], b_ss.at[k - 1, step], b_rs.at[k - 1, to])
            sums = sums + brecv[k - 1, to].astype(F32)
        if step:
            b2send[step - 1] = sums.astype(BF16)
            send(b2send.at[step - 1], b2recv.at[step - 1], b2_ss.at[step - 1], b2_rs.at[step - 1], xdev(step, c))
        else:
            second_half = sums
    for step in range(1, NY):
        arrived(a2recv.at[step - 1], a2_ss.at[step - 1], a2_rs.at[step - 1])
        first_half = first_half + a2recv[step - 1].astype(F32)
    for step in range(1, NX):
        arrived(b2recv.at[step - 1], b2_ss.at[step - 1], b2_rs.at[step - 1])
        second_half = second_half + b2recv[step - 1].astype(F32)

    for k in range(NZ // 2):
        zpart[2 * k] = first_half[8 * k : 8 * k + 8]
        zpart[2 * k + 1] = second_half[8 * k : 8 * k + 8]
    zsend[...] = zpart[...].astype(BF16)
    for step in order:
        to = lax.rem(z + step, NZ)
        send(zsend.at[to], zrecv.at[step - 1], z_ss.at[step - 1], z_rs.at[step - 1], zdev(step))

    eye = lax.broadcasted_iota(jnp.int32, (CENT, CENT), 0) == lax.broadcasted_iota(jnp.int32, (CENT, CENT), 1)
    count_column = jnp.sum(jnp.where(eye, totals[0][:, 0:CENT], 0.0), axis=1, keepdims=True)
    done = ((joined(0) + received(4) + received(6)) / count_column).astype(BF16)
    fc_out[...] = done
    xg[c, x] = done
    for step in range(1, NX):
        send(xg.at[c, x], xg.at[c, x], x_ss.at[step - 1], x_rs.at[step - 1], xdev(step, c))
    counts = zcsend[...]
    for step in range(1, NZ):
        arrived(zcrecv.at[step - 1], zc_ss.at[step - 1], zc_rs.at[step - 1])
        counts = counts + zcrecv[step - 1]
    drain()
    eight = lax.broadcasted_iota(jnp.int32, (8, 128), 0) + (z // 2) * 8 == lax.broadcasted_iota(jnp.int32, (8, 128), 1)
    second_counts = jnp.sum(jnp.where(eight, counts, 0.0), axis=1, keepdims=True)
    sums = zpart[z]
    for step in reversed(order):
        arrived(zrecv.at[step - 1], z_ss.at[step - 1], z_rs.at[step - 1])
        sums = sums + zrecv[step - 1].astype(F32)
    second = (sums / second_counts).astype(BF16)
    pair, side = z // 2, lax.rem(z, 2)
    zg[pair, side] = second
    for step in order:
        send(zg.at[pair, side], zg.at[pair, side], za_ss.at[step - 1], za_rs.at[step - 1], zdev(step))
    scorer = y // (NY // 2)
    slot = lax.rem(y, NY // 2)
    drain()
    for step in range(1, NX):
        source = lax.rem(x + NX - step, NX)
        arrived(xg.at[c, source], x_ss.at[step - 1], x_rs.at[step - 1])
    send(xg.at[c], xg.at[c], pt_ss, pt_rs, partner)
    for d in (0, 1, 7, 2, 6, 3, 5, 4):
        there = lax.rem(pair + d, NZ // 2)
        for h in range(2):
            source = 2 * there + h
            step = lax.rem(z + NZ - source, NZ)
            if d:
                arrived(zg.at[there, h], za_ss.at[0], za_rs.at[step - 1])
        if not d:
            step = lax.rem(NZ + 2 * side - 1, NZ)
            arrived(zg.at[pair, 1 - side], za_ss.at[0], za_rs.at[step - 1])
            ours = zg[pair].astype(F32)
            for h in range(2):
                rows = jnp.where(side == 0, ours[h, 0:4], ours[h, 4:8])
                sc_out[:, pl.ds(h * fold, fold)] = rows.astype(BF16)
        for k in range(1, NY):
            send(zg.at[there], yg.at[c, slot, there], ya_ss.at[k - 1, d], ya_rs.at[c, slot], ydev(k, scorer))
    own_scorer = scorer == c
    to_scorer = pltpu.make_async_remote_copy(
        src_ref=zg, dst_ref=yg.at[c, slot], send_sem=pg_ss, recv_sem=ya_rs.at[c, slot],
        device_id=partner, device_id_type=MESH,
    )

    @pl.when(own_scorer)
    def _():
        yg[c, slot] = zg[...]

    @pl.when(jnp.logical_not(own_scorer))
    def _():
        to_scorer.start()

    arrived(xg.at[1 - c], pt_ss, pt_rs)
    for s in range(NY // 2):
        for k in range(2):
            here = jnp.logical_and(c * (NY // 2) + s == y, c == k)

            @pl.when(jnp.logical_not(here))
            def _():
                arrived(yg.at[k, s], pg_ss, ya_rs.at[k, s])

    groups = NY // 2 * quarter
    scores = jnp.zeros((NX * CENT, groups), F32)
    squares = jnp.zeros((groups, 1), F32)
    for k in range(2):
        for h in range(2):
            b = yg[k, :, :, h].reshape(groups, fold)
            scores = scores + dot_nt(xg[k, :, :, pl.ds(h * fold, fold)].reshape(NX * CENT, fold), b)
            b32 = b.astype(F32)
            squares = squares + jnp.sum(b32 * b32, axis=1, keepdims=True)
    eye = lax.broadcasted_iota(jnp.int32, (groups, groups), 0) == lax.broadcasted_iota(jnp.int32, (groups, groups), 1)
    norm_row = jnp.sum(jnp.where(eye, squares, 0.0), axis=0, keepdims=True)
    ssend[...] = (scores - 0.5 * norm_row).astype(BF16).reshape(NX, CENT, groups)
    holder = x // (NX // 2)
    out_slot = lax.rem(x, NX // 2) * 2 + c
    for step in range(1, NX):
        to = lax.rem(x + step, NX)
        send(ssend.at[to], sret.at[out_slot], r_ss.at[step], r_rs.at[out_slot], xdev(step, holder))
    own_holder = holder == c
    to_holder = pltpu.make_async_remote_copy(
        src_ref=ssend.at[x], dst_ref=sret.at[out_slot], send_sem=r_ss.at[0], recv_sem=r_rs.at[out_slot],
        device_id=partner, device_id_type=MESH,
    )

    @pl.when(own_holder)
    def _():
        sret[out_slot] = ssend[x]

    @pl.when(jnp.logical_not(own_holder))
    def _():
        to_holder.start()

    drain()

    @pl.when(jnp.logical_not(own_scorer))
    def _():
        to_scorer.wait_send()

    @pl.when(jnp.logical_not(own_holder))
    def _():
        to_holder.wait_send()

    for s in range(NX):
        here = jnp.logical_and(c * (NX // 2) + s // 2 == x, c == s % 2)

        @pl.when(jnp.logical_not(here))
        def _():
            arrived(sret.at[s], r_ss.at[0], r_rs.at[s])


def write_out(fc, sc, sret, fc_out, sc_out, scores_out, wide, sems):
    copies = [
        pltpu.make_async_copy(fc, fc_out, sems.at[0]),
        pltpu.make_async_copy(sc, sc_out, sems.at[1]),
    ]
    for copy in copies:
        copy.start()
    groups = sret.shape[2]
    for s in range(NX):
        wide[:, pl.ds(s * groups, groups)] = sret[s].astype(F32)
    copies.append(pltpu.make_async_copy(wide, scores_out, sems.at[2]))
    copies[2].start()
    for copy in copies:
        copy.wait()


def shards(embeddings, first_level, second_level):
    dma = pltpu.SemaphoreType.DMA
    quarter = NZ * 4
    groups = NY // 2 * quarter
    fold = HALF // 2
    vmem = pl.BlockSpec(memory_space=pltpu.VMEM)
    hbm = pl.BlockSpec(memory_space=pltpu.HBM)
    operands = (embeddings, first_level.reshape(1, ROWS), second_level.reshape(1, CENT))
    first, second, returned = pl.pallas_call(
        kernel,
        out_shape=(
            jax.ShapeDtypeStruct((CENT, HALF), BF16),
            jax.ShapeDtypeStruct((4, HALF), BF16),
            jax.ShapeDtypeStruct((NX, CENT, groups), BF16),
        ),
        in_specs=[hbm] * 3,
        out_specs=(vmem,) * 3,
        scratch_shapes=[
            pltpu.VMEM((1, ROWS), jnp.int32),
            pltpu.VMEM((1, CENT), jnp.int32),
            pltpu.VMEM((ROWS, HALF), BF16),
            pltpu.VMEM((BAND * CENT, ROWS), BF16),
            pltpu.VMEM((BAND * CENT, HALF), F32),
            pltpu.VMEM((BAND * CENT, HALF), BF16),
            pltpu.VMEM((3, CENT, HALF), BF16),
            pltpu.VMEM((BAND - 1, CENT, HALF), BF16),
            pltpu.VMEM((BAND, 1, 128), F32),
            pltpu.VMEM((2 * BAND - 1, BAND, 1, 128), F32),
            pltpu.VMEM((2, NX, CENT, HALF), BF16),
            pltpu.VMEM((NX, 1, 128), jnp.int32),
            pltpu.VMEM((NX - 1, NY, quarter, fold), BF16),
            pltpu.VMEM((NX - 1, NY, quarter, fold), BF16),
            pltpu.VMEM((NX, NY, quarter, fold), F32),
            pltpu.VMEM((NY - 1, NX, quarter, fold), BF16),
            pltpu.VMEM((NY - 1, NX, quarter, fold), BF16),
            pltpu.VMEM((NY, NX, quarter, fold), F32),
            pltpu.VMEM((NY - 1, quarter, fold), BF16),
            pltpu.VMEM((NY - 1, quarter, fold), BF16),
            pltpu.VMEM((NX - 1, quarter, fold), BF16),
            pltpu.VMEM((NX - 1, quarter, fold), BF16),
            pltpu.VMEM((NY, 1, 128), F32),
            pltpu.VMEM((NY - 1, 1, 128), F32),
            pltpu.VMEM((1, 128), F32),
            pltpu.VMEM((NZ - 1, 1, 128), F32),
            pltpu.VMEM((NZ, 8, fold), BF16),
            pltpu.VMEM((NZ, 8, fold), F32),
            pltpu.VMEM((NZ - 1, 8, fold), BF16),
            pltpu.VMEM((NZ // 2, 2, 8, fold), BF16),
            pltpu.VMEM((2, NY // 2, NZ // 2, 2, 8, fold), BF16),
            pltpu.VMEM((NX, CENT, groups), BF16),
            dma, dma, dma,
            dma((2 * BAND - 1,)), dma((2 * BAND - 1,)),
            dma((BAND - 1,)), dma((BAND - 1,)),
            dma((NX - 1,)), dma((NX - 1,)),
            dma((NX - 1,)), dma((NX - 1,)),
            dma, dma,
            dma((NX - 1, NY)), dma((NX - 1, NY)),
            dma((NY - 1, NX)), dma((NY - 1, NX)),
            dma((NY - 1,)), dma((NY - 1,)),
            dma((NX - 1,)), dma((NX - 1,)),
            dma((NY - 1,)), dma((NY - 1,)),
            dma((NZ - 1,)), dma((NZ - 1,)),
            dma((NZ - 1,)), dma((NZ - 1,)),
            dma((NZ - 1,)), dma((NZ - 1,)),
            dma((NY - 1, NZ // 2)), dma((2, NY // 2)), dma,
            dma((NX,)), dma((NX,)),
        ],
        compiler_params=pltpu.CompilerParams(
            collective_id=0, has_side_effects=True, vmem_limit_bytes=40 << 20
        ),
        name="update",
    )(*(pltpu.with_memory_space_constraint(a, pltpu.HBM) for a in operands))
    return pl.pallas_call(
        write_out,
        out_shape=(
            jax.ShapeDtypeStruct((CENT, HALF), BF16),
            jax.ShapeDtypeStruct((4, HALF), BF16),
            jax.ShapeDtypeStruct((CENT, HALF), F32),
        ),
        in_specs=[vmem] * 3,
        out_specs=(hbm,) * 3,
        scratch_shapes=[pltpu.VMEM((CENT, HALF), F32), dma((3,))],
        compiler_params=pltpu.CompilerParams(vmem_limit_bytes=8 << 20),
        name="write_out",
    )(first, second, returned)


def solution(mesh):
    torus = Mesh(mesh.devices.reshape(NX, NY, NZ, mesh.shape["mp"]), (*DP, "mp"))
    return jax.shard_map(
        shards,
        mesh=torus,
        in_specs=(P(DP, "mp"), P(DP), P(DP, None)),
        out_specs=(P(DP, "mp"), P(DP, "mp"), P(DP, "mp")),
        check_vma=False,
    )
```

```python
import jax
import jax.numpy as jnp
from jax import lax
from jax.experimental import pallas as pl
from jax.experimental.pallas import tpu as pltpu
from jax.sharding import Mesh
from jax.sharding import PartitionSpec as P

NX, NY, NZ = 4, 4, 16
CENT = 64
BAND = 8
ROWS = 3072
HALF = 512
K1 = 16384
DP = ("dp_0", "dp_1", "dp_2")
MESH = pl.DeviceIdType.MESH
F32 = jnp.float32
BF16 = jnp.bfloat16


def dot_nt(a, b):
    return lax.dot_general(a, b, (((1,), (1,)), ((), ())), preferred_element_type=F32)


def kernel(
    emb_hbm, ids_hbm, sec_hbm,
    fc_out, sc_out, sret,
    ids_ref, sec_ref, emb, oh, part, partb, csend, crecv, table, tables, xg, idbuf,
    asend, arecv, apart, bsend, brecv, bpart, a2send, a2recv, b2send, b2recv,
    ycsend, ycrecv, zcsend, zcrecv, zsend, zpart, zrecv, zg, yg, ssend,
    emb_sem, ids_sem, sec_sem, t_ss, t_rs, c_ss, c_rs, x_ss, x_rs, id_ss, id_rs, pt_ss, pt_rs,
    a_ss, a_rs, b_ss, b_rs, a2_ss, a2_rs, b2_ss, b2_rs,
    yc_ss, yc_rs, zc_ss, zc_rs, z_ss, z_rs, za_ss, za_rs, ya_ss, ya_rs, pg_ss, r_ss, r_rs,
):
    x = lax.axis_index("dp_0")
    y = lax.axis_index("dp_1")
    z = lax.axis_index("dp_2")
    c = lax.axis_index("mp")
    me = (x * NY + y) * NZ + z
    devices = NX * NY * NZ

    def chip(step):
        index = lax.rem(me + step + devices, devices)
        return (index // (NY * NZ), lax.rem(index // NZ, NY), lax.rem(index, NZ), c)

    def xdev(step, core):
        return (lax.rem(x + step, NX), y, z, core)

    def ydev(step, core):
        return (x, lax.rem(y + step, NY), z, core)

    def zdev(step):
        return (x, y, lax.rem(z + step, NZ), c)

    partner = (x, y, z, 1 - c)
    load_ids = pltpu.make_async_copy(ids_hbm, ids_ref, ids_sem)
    load_sec = pltpu.make_async_copy(sec_hbm, sec_ref, sec_sem)
    load = pltpu.make_async_copy(emb_hbm, emb, emb_sem)
    load_ids.start()
    load_sec.start()
    load.start()

    barrier = pltpu.get_barrier_semaphore()
    near = [d for k in range(1, BAND) for d in (k, -k)]
    peers = [partner] + [chip(d) for d in near]
    for step in range(1, NX):
        peers += [xdev(step, 0), xdev(step, 1)]
    for step in range(1, NY):
        peers += [ydev(step, 0), ydev(step, 1)]
    for step in range(1, NZ):
        peers.append(zdev(step))
    for peer in peers:
        pl.semaphore_signal(barrier, inc=1, device_id=peer, device_id_type=MESH)

    pending = []

    def send(src, dst, ssem, rsem, device):
        copy = pltpu.make_async_remote_copy(
            src_ref=src, dst_ref=dst, send_sem=ssem, recv_sem=rsem, device_id=device, device_id_type=MESH
        )
        copy.start()
        pending.append(copy)

    def drain():
        while pending:
            pending.pop(0).wait_send()

    def arrived(dst, ssem, rsem):
        pltpu.make_async_remote_copy(
            src_ref=dst, dst_ref=dst, send_sem=ssem, recv_sem=rsem, device_id=partner, device_id_type=MESH
        ).wait_recv()

    load_ids.wait()
    shifted = ids_ref[...] - me * CENT
    local = jnp.where(shifted < 0, shifted + K1, shifted)
    ones_row = jnp.ones((8, 128), BF16)
    load_sec.wait()
    table[...] = jnp.zeros_like(table)
    table[0, :, pl.ds(CENT, CENT)] = sec_ref[...].astype(F32)
    idbuf[x, :, pl.ds(0, CENT)] = sec_ref[...]
    idbuf[x, :, pl.ds(CENT, CENT)] = sec_ref[...]
    for j in range(BAND):
        rows = pl.ds(j * CENT, CENT)
        wanted = lax.broadcasted_iota(jnp.int32, (CENT, ROWS), 0) + j * CENT
        oh[rows, :] = jnp.where(local == wanted, 1.0, 0.0).astype(BF16)
        folded = oh[rows, pl.ds(0, 128)]
        for k in range(1, ROWS // 128):
            folded = folded + oh[rows, pl.ds(k * 128, 128)]
        table[j, :, pl.ds(0, CENT)] = dot_nt(ones_row, folded)[0:1]

    pl.semaphore_wait(barrier, len(peers))

    for d in near:
        kept = pl.ds(d, BAND - d) if d > 0 else pl.ds(0, BAND + d)
        t = d + BAND - 1
        send(table.at[kept], tables.at[t, kept], t_ss.at[t], t_rs.at[t], chip(d))
    for step in range(1, NX):
        send(idbuf.at[x], idbuf.at[x], id_ss.at[step - 1], id_rs.at[step - 1], xdev(step, c))

    def band(j):
        return pl.ds(j * CENT, CENT)

    def step_one(q):
        send(partb.at[band(2 * q + 1)], crecv.at[q], c_ss.at[q], c_rs.at[q], chip(1))

    def joined(j):
        arrived(crecv.at[j // 2], c_ss.at[j // 2], c_rs.at[j // 2])
        return part[band(j), :] + crecv[j // 2].astype(F32)

    def step_two(j):
        k = 4 + j // 4
        csend[k - 4] = joined(j).astype(BF16)
        send(csend.at[k - 4], crecv.at[k], c_ss.at[k], c_rs.at[k], chip(2))

    def received(k):
        arrived(crecv.at[k], c_ss.at[k], c_rs.at[k])
        return crecv[k].astype(F32)

    def step_three():
        csend[2] = (joined(4) + received(5)).astype(BF16)
        send(csend.at[2], crecv.at[6], c_ss.at[6], c_rs.at[6], chip(4))

    half = BAND // 2 * CENT
    load.wait()
    for begin in (half, 0):
        rows = pl.ds(begin, half)
        sums = jnp.dot(oh[rows, :], emb[...], preferred_element_type=F32)
        part[rows, :] = sums
        partb[rows, :] = sums.astype(BF16)
        if begin:
            pass

    step_one(3)
    step_one(1)
    step_one(2)
    step_one(0)
    for step in range(1, NX):
        arrived(idbuf.at[lax.rem(x + NX - step, NX)], id_ss.at[step - 1], id_rs.at[step - 1])
    lane = lax.broadcasted_iota(jnp.int32, (1, 128), 1)
    block = NY * NZ * 4
    quarter = NZ * 4
    group = lax.broadcasted_iota(jnp.int32, (block, 128), 0) + x * block
    hits = []
    for pair in range(NX // 2):
        names = jnp.where(lane < CENT, idbuf[2 * pair], idbuf[2 * pair + 1])
        hits.append(jnp.where(names == group, 1.0, 0.0))
    hit = (hits[0] + hits[1]).astype(BF16)
    ycsend[...] = jnp.zeros_like(ycsend)
    for k in range(NY):
        ycsend[k, :, pl.ds(0, CENT)] = dot_nt(ones_row, hit[k * quarter : (k + 1) * quarter])[0:1]
    for step in range(1, NY):
        to = lax.rem(y + step, NY)
        send(ycsend.at[to], ycrecv.at[step - 1], yc_ss.at[step - 1], yc_rs.at[step - 1], ydev(step, c))

    for d in near:
        kept = pl.ds(d, BAND - d) if d > 0 else pl.ds(0, BAND + d)
        t = d + BAND - 1
        arrived(tables.at[t, kept], t_ss.at[t], t_rs.at[t])
    totals, name_rows = [], []
    for j in range(BAND):
        total = table[j]
        for d in near:
            k = j + d
            if 0 <= k < BAND:
                total = total + tables[d + BAND - 1, k]
        totals.append(total)
        name_rows.append(table[0] if j == 0 else tables[BAND - 1 - j, 0])
    names, weights = [], []
    for k in range(BAND // 2):
        names.append(jnp.where(lane < CENT, pltpu.roll(name_rows[2 * k], CENT, 1), name_rows[2 * k + 1]))
        weights.append(1.0 / jnp.where(lane < CENT, totals[2 * k], pltpu.roll(totals[2 * k + 1], CENT, 1)))
    names = jnp.concatenate(names, axis=1).astype(jnp.int32)
    weights = jnp.concatenate(weights, axis=1)

    fold = HALF // 2
    far_x = [2, 1, 3, 0]
    far_y = [2, 1, 3, 0]
    for step in far_x:
        to = lax.rem(x + step, NX)
        wanted = lax.broadcasted_iota(jnp.int32, (block, BAND * CENT), 0) + to * block
        member = jnp.where(names == wanted, weights, 0.0).astype(BF16)
        sums = jnp.dot(member, partb[...], preferred_element_type=F32)
        for k in range(NY):
            apart[step, k] = sums[k * quarter : (k + 1) * quarter, :fold]
            bpart[k, to] = sums[k * quarter : (k + 1) * quarter, fold:]
        if step:
            asend[step - 1] = sums[:, :fold].reshape(NY, quarter, fold).astype(BF16)
        for k in far_y:
            at = lax.rem(y + k, NY)
            if step:
                send(
                    asend.at[step - 1, at], arecv.at[step - 1, at],
                    a_ss.at[step - 1, k], a_rs.at[step - 1, k], xdev(step, c),
                )
            if k:
                bsend[k - 1, step] = bpart[at, to].astype(BF16)
                send(
                    bsend.at[k - 1, step], brecv.at[k - 1, to],
                    b_ss.at[k - 1, step], b_rs.at[k - 1, to], ydev(k, c),
                )
    line = ycsend[y]
    for step in range(1, NY):
        arrived(ycrecv.at[step - 1], yc_ss.at[step - 1], yc_rs.at[step - 1])
        line = line + ycrecv[step - 1]
    zcsend[...] = line
    order = sorted(range(1, NZ), key=lambda step: -min(step, NZ - step))
    for step in order:
        send(zcsend, zcrecv.at[step - 1], zc_ss.at[step - 1], zc_rs.at[step - 1], zdev(step))
    step_two(6)

    for t in range(NY):
        step = far_y[t]
        to = lax.rem(y + step, NY)
        sums = apart[0, to]
        for k in range(1, NX):
            arrived(arecv.at[k - 1, to], a_ss.at[k - 1, step], a_rs.at[k - 1, step])
            sums = sums + arecv[k - 1, to].astype(F32)
        if step:
            a2send[step - 1] = sums.astype(BF16)
            send(a2send.at[step - 1], a2recv.at[step - 1], a2_ss.at[step - 1], a2_rs.at[step - 1], ydev(step, c))
        else:
            first_half = sums
        step = far_x[t]
        to = lax.rem(x + step, NX)
        sums = bpart[y, to]
        for k in range(1, NY):
            arrived(brecv.at[k - 1, to], b_ss.at[k - 1, step], b_rs.at[k - 1, to])
            sums = sums + brecv[k - 1, to].astype(F32)
        if step:
            b2send[step - 1] = sums.astype(BF16)
            send(b2send.at[step - 1], b2recv.at[step - 1], b2_ss.at[step - 1], b2_rs.at[step - 1], xdev(step, c))
        else:
            second_half = sums
    step_two(2)
    for step in range(1, NY):
        arrived(a2recv.at[step - 1], a2_ss.at[step - 1], a2_rs.at[step - 1])
        first_half = first_half + a2recv[step - 1].astype(F32)
    for step in range(1, NX):
        arrived(b2recv.at[step - 1], b2_ss.at[step - 1], b2_rs.at[step - 1])
        second_half = second_half + b2recv[step - 1].astype(F32)

    for k in range(NZ // 2):
        zpart[2 * k] = first_half[8 * k : 8 * k + 8]
        zpart[2 * k + 1] = second_half[8 * k : 8 * k + 8]
    zsend[...] = zpart[...].astype(BF16)
    for step in order:
        to = lax.rem(z + step, NZ)
        send(zsend.at[to], zrecv.at[step - 1], z_ss.at[step - 1], z_rs.at[step - 1], zdev(step))

    step_three()
    counts = zcsend[...]
    for step in range(1, NZ):
        arrived(zcrecv.at[step - 1], zc_ss.at[step - 1], zc_rs.at[step - 1])
        counts = counts + zcrecv[step - 1]
    drain()
    eight = lax.broadcasted_iota(jnp.int32, (8, 128), 0) + (z // 2) * 8 == lax.broadcasted_iota(jnp.int32, (8, 128), 1)
    second_counts = jnp.sum(jnp.where(eight, counts, 0.0), axis=1, keepdims=True)
    sums = zpart[z]
    for step in reversed(order):
        arrived(zrecv.at[step - 1], z_ss.at[step - 1], z_rs.at[step - 1])
        sums = sums + zrecv[step - 1].astype(F32)
    second = (sums / second_counts).astype(BF16)
    pair, side = z // 2, lax.rem(z, 2)
    zg[pair, side] = second
    for step in order:
        send(zg.at[pair, side], zg.at[pair, side], za_ss.at[step - 1], za_rs.at[step - 1], zdev(step))
    scorer = y // (NY // 2)
    slot = lax.rem(y, NY // 2)
    eye = lax.broadcasted_iota(jnp.int32, (CENT, CENT), 0) == lax.broadcasted_iota(jnp.int32, (CENT, CENT), 1)
    count_column = jnp.sum(jnp.where(eye, totals[0][:, 0:CENT], 0.0), axis=1, keepdims=True)
    done = ((joined(0) + received(4) + received(6)) / count_column).astype(BF16)
    fc_out[...] = done
    xg[c, x] = done
    for step in range(1, NX):
        send(xg.at[c, x], xg.at[c, x], x_ss.at[step - 1], x_rs.at[step - 1], xdev(step, c))
    drain()
    for d in (0, 1, 7, 2, 6, 3, 5, 4):
        there = lax.rem(pair + d, NZ // 2)
        for h in range(2):
            source = 2 * there + h
            step = lax.rem(z + NZ - source, NZ)
            if d:
                arrived(zg.at[there, h], za_ss.at[0], za_rs.at[step - 1])
        if not d:
            step = lax.rem(NZ + 2 * side - 1, NZ)
            arrived(zg.at[pair, 1 - side], za_ss.at[0], za_rs.at[step - 1])
            ours = zg[pair].astype(F32)
            for h in range(2):
                rows = jnp.where(side == 0, ours[h, 0:4], ours[h, 4:8])
                sc_out[:, pl.ds(h * fold, fold)] = rows.astype(BF16)
        for k in range(1, NY):
            send(zg.at[there], yg.at[c, slot, there], ya_ss.at[k - 1, d], ya_rs.at[c, slot], ydev(k, scorer))
    own_scorer = scorer == c
    to_scorer = pltpu.make_async_remote_copy(
        src_ref=zg, dst_ref=yg.at[c, slot], send_sem=pg_ss, recv_sem=ya_rs.at[c, slot],
        device_id=partner, device_id_type=MESH,
    )

    @pl.when(own_scorer)
    def _():
        yg[c, slot] = zg[...]

    @pl.when(jnp.logical_not(own_scorer))
    def _():
        to_scorer.start()

    for step in range(1, NX):
        source = lax.rem(x + NX - step, NX)
        arrived(xg.at[c, source], x_ss.at[step - 1], x_rs.at[step - 1])
    send(xg.at[c], xg.at[c], pt_ss, pt_rs, partner)
    arrived(xg.at[1 - c], pt_ss, pt_rs)
    for s in range(NY // 2):
        for k in range(2):
            here = jnp.logical_and(c * (NY // 2) + s == y, c == k)

            @pl.when(jnp.logical_not(here))
            def _():
                arrived(yg.at[k, s], pg_ss, ya_rs.at[k, s])

    groups = NY // 2 * quarter
    scores = jnp.zeros((NX * CENT, groups), F32)
    squares = jnp.zeros((groups, 1), F32)
    for k in range(2):
        for h in range(2):
            b = yg[k, :, :, h].reshape(groups, fold)
            scores = scores + dot_nt(xg[k, :, :, pl.ds(h * fold, fold)].reshape(NX * CENT, fold), b)
            b32 = b.astype(F32)
            squares = squares + jnp.sum(b32 * b32, axis=1, keepdims=True)
    eye = lax.broadcasted_iota(jnp.int32, (groups, groups), 0) == lax.broadcasted_iota(jnp.int32, (groups, groups), 1)
    norm_row = jnp.sum(jnp.where(eye, squares, 0.0), axis=0, keepdims=True)
    ssend[...] = (scores - 0.5 * norm_row).astype(BF16).reshape(NX, CENT, groups)
    holder = x // (NX // 2)
    out_slot = lax.rem(x, NX // 2) * 2 + c
    for step in range(1, NX):
        to = lax.rem(x + step, NX)
        send(ssend.at[to], sret.at[out_slot], r_ss.at[step], r_rs.at[out_slot], xdev(step, holder))
    own_holder = holder == c
    to_holder = pltpu.make_async_remote_copy(
        src_ref=ssend.at[x], dst_ref=sret.at[out_slot], send_sem=r_ss.at[0], recv_sem=r_rs.at[out_slot],
        device_id=partner, device_id_type=MESH,
    )

    @pl.when(own_holder)
    def _():
        sret[out_slot] = ssend[x]

    @pl.when(jnp.logical_not(own_holder))
    def _():
        to_holder.start()

    drain()

    @pl.when(jnp.logical_not(own_scorer))
    def _():
        to_scorer.wait_send()

    @pl.when(jnp.logical_not(own_holder))
    def _():
        to_holder.wait_send()

    for s in range(NX):
        here = jnp.logical_and(c * (NX // 2) + s // 2 == x, c == s % 2)

        @pl.when(jnp.logical_not(here))
        def _():
            arrived(sret.at[s], r_ss.at[0], r_rs.at[s])


def write_out(fc, sc, sret, fc_out, sc_out, scores_out, wide, sems):
    copies = [
        pltpu.make_async_copy(fc, fc_out, sems.at[0]),
        pltpu.make_async_copy(sc, sc_out, sems.at[1]),
    ]
    for copy in copies:
        copy.start()
    groups = sret.shape[2]
    for s in range(NX):
        wide[:, pl.ds(s * groups, groups)] = sret[s].astype(F32)
    copies.append(pltpu.make_async_copy(wide, scores_out, sems.at[2]))
    copies[2].start()
    for copy in copies:
        copy.wait()


def shards(embeddings, first_level, second_level):
    dma = pltpu.SemaphoreType.DMA
    quarter = NZ * 4
    groups = NY // 2 * quarter
    fold = HALF // 2
    vmem = pl.BlockSpec(memory_space=pltpu.VMEM)
    hbm = pl.BlockSpec(memory_space=pltpu.HBM)
    operands = (embeddings, first_level.reshape(1, ROWS), second_level.reshape(1, CENT))
    first, second, returned = pl.pallas_call(
        kernel,
        out_shape=(
            jax.ShapeDtypeStruct((CENT, HALF), BF16),
            jax.ShapeDtypeStruct((4, HALF), BF16),
            jax.ShapeDtypeStruct((NX, CENT, groups), BF16),
        ),
        in_specs=[hbm] * 3,
        out_specs=(vmem,) * 3,
        scratch_shapes=[
            pltpu.VMEM((1, ROWS), jnp.int32),
            pltpu.VMEM((1, CENT), jnp.int32),
            pltpu.VMEM((ROWS, HALF), BF16),
            pltpu.VMEM((BAND * CENT, ROWS), BF16),
            pltpu.VMEM((BAND * CENT, HALF), F32),
            pltpu.VMEM((BAND * CENT, HALF), BF16),
            pltpu.VMEM((3, CENT, HALF), BF16),
            pltpu.VMEM((BAND - 1, CENT, HALF), BF16),
            pltpu.VMEM((BAND, 1, 128), F32),
            pltpu.VMEM((2 * BAND - 1, BAND, 1, 128), F32),
            pltpu.VMEM((2, NX, CENT, HALF), BF16),
            pltpu.VMEM((NX, 1, 128), jnp.int32),
            pltpu.VMEM((NX - 1, NY, quarter, fold), BF16),
            pltpu.VMEM((NX - 1, NY, quarter, fold), BF16),
            pltpu.VMEM((NX, NY, quarter, fold), F32),
            pltpu.VMEM((NY - 1, NX, quarter, fold), BF16),
            pltpu.VMEM((NY - 1, NX, quarter, fold), BF16),
            pltpu.VMEM((NY, NX, quarter, fold), F32),
            pltpu.VMEM((NY - 1, quarter, fold), BF16),
            pltpu.VMEM((NY - 1, quarter, fold), BF16),
            pltpu.VMEM((NX - 1, quarter, fold), BF16),
            pltpu.VMEM((NX - 1, quarter, fold), BF16),
            pltpu.VMEM((NY, 1, 128), F32),
            pltpu.VMEM((NY - 1, 1, 128), F32),
            pltpu.VMEM((1, 128), F32),
            pltpu.VMEM((NZ - 1, 1, 128), F32),
            pltpu.VMEM((NZ, 8, fold), BF16),
            pltpu.VMEM((NZ, 8, fold), F32),
            pltpu.VMEM((NZ - 1, 8, fold), BF16),
            pltpu.VMEM((NZ // 2, 2, 8, fold), BF16),
            pltpu.VMEM((2, NY // 2, NZ // 2, 2, 8, fold), BF16),
            pltpu.VMEM((NX, CENT, groups), BF16),
            dma, dma, dma,
            dma((2 * BAND - 1,)), dma((2 * BAND - 1,)),
            dma((BAND - 1,)), dma((BAND - 1,)),
            dma((NX - 1,)), dma((NX - 1,)),
            dma((NX - 1,)), dma((NX - 1,)),
            dma, dma,
            dma((NX - 1, NY)), dma((NX - 1, NY)),
            dma((NY - 1, NX)), dma((NY - 1, NX)),
            dma((NY - 1,)), dma((NY - 1,)),
            dma((NX - 1,)), dma((NX - 1,)),
            dma((NY - 1,)), dma((NY - 1,)),
            dma((NZ - 1,)), dma((NZ - 1,)),
            dma((NZ - 1,)), dma((NZ - 1,)),
            dma((NZ - 1,)), dma((NZ - 1,)),
            dma((NY - 1, NZ // 2)), dma((2, NY // 2)), dma,
            dma((NX,)), dma((NX,)),
        ],
        compiler_params=pltpu.CompilerParams(
            collective_id=0, has_side_effects=True, vmem_limit_bytes=40 << 20
        ),
        name="update",
    )(*(pltpu.with_memory_space_constraint(a, pltpu.HBM) for a in operands))
    return pl.pallas_call(
        write_out,
        out_shape=(
            jax.ShapeDtypeStruct((CENT, HALF), BF16),
            jax.ShapeDtypeStruct((4, HALF), BF16),
            jax.ShapeDtypeStruct((CENT, HALF), F32),
        ),
        in_specs=[vmem] * 3,
        out_specs=(hbm,) * 3,
        scratch_shapes=[pltpu.VMEM((CENT, HALF), F32), dma((3,))],
        compiler_params=pltpu.CompilerParams(vmem_limit_bytes=8 << 20),
        name="write_out",
    )(first, second, returned)


def solution(mesh):
    torus = Mesh(mesh.devices.reshape(NX, NY, NZ, mesh.shape["mp"]), (*DP, "mp"))
    return jax.shard_map(
        shards,
        mesh=torus,
        in_specs=(P(DP, "mp"), P(DP), P(DP, None)),
        out_specs=(P(DP, "mp"), P(DP, "mp"), P(DP, "mp")),
        check_vma=False,
    )
```

```python
import jax
import jax.numpy as jnp
from jax import lax
from jax.experimental import pallas as pl
from jax.experimental.pallas import tpu as pltpu
from jax.sharding import Mesh
from jax.sharding import PartitionSpec as P

NX, NY, NZ = 4, 4, 16
CENT = 64
BAND = 8
ROWS = 3072
HALF = 512
K1 = 16384
DP = ("dp_0", "dp_1", "dp_2")
MESH = pl.DeviceIdType.MESH
F32 = jnp.float32
BF16 = jnp.bfloat16


def dot_nt(a, b):
    return lax.dot_general(a, b, (((1,), (1,)), ((), ())), preferred_element_type=F32)


def kernel(
    emb_hbm, ids_hbm, sec_hbm,
    fc_out, sc_out, sret,
    ids_ref, sec_ref, emb, oh, part, partb, csend, crecv, table, tables, xg, idbuf,
    asend, arecv, apart, bsend, brecv, bpart, a2send, a2recv, b2send, b2recv,
    ycsend, ycrecv, zcsend, zcrecv, zsend, zpart, zrecv, zg, yg, ssend,
    emb_sem, ids_sem, sec_sem, t_ss, t_rs, c_ss, c_rs, x_ss, x_rs, id_ss, id_rs, pt_ss, pt_rs,
    a_ss, a_rs, b_ss, b_rs, a2_ss, a2_rs, b2_ss, b2_rs,
    yc_ss, yc_rs, zc_ss, zc_rs, z_ss, z_rs, za_ss, za_rs, ya_ss, ya_rs, pg_ss, r_ss, r_rs,
):
    x = lax.axis_index("dp_0")
    y = lax.axis_index("dp_1")
    z = lax.axis_index("dp_2")
    c = lax.axis_index("mp")
    me = (x * NY + y) * NZ + z
    devices = NX * NY * NZ

    def chip(step):
        index = lax.rem(me + step + devices, devices)
        return (index // (NY * NZ), lax.rem(index // NZ, NY), lax.rem(index, NZ), c)

    def xdev(step, core):
        return (lax.rem(x + step, NX), y, z, core)

    def ydev(step, core):
        return (x, lax.rem(y + step, NY), z, core)

    def zdev(step):
        return (x, y, lax.rem(z + step, NZ), c)

    partner = (x, y, z, 1 - c)
    load_ids = pltpu.make_async_copy(ids_hbm, ids_ref, ids_sem)
    load_sec = pltpu.make_async_copy(sec_hbm, sec_ref, sec_sem)
    load = pltpu.make_async_copy(emb_hbm, emb, emb_sem)
    load_ids.start()
    load_sec.start()
    load.start()

    barrier = pltpu.get_barrier_semaphore()
    near = [d for k in range(1, BAND) for d in (k, -k)]
    peers = [partner] + [chip(d) for d in near]
    for step in range(1, NX):
        peers += [xdev(step, 0), xdev(step, 1)]
    for step in range(1, NY):
        peers += [ydev(step, 0), ydev(step, 1)]
    for step in range(1, NZ):
        peers.append(zdev(step))
    for peer in reversed(peers):
        pl.semaphore_signal(barrier, inc=1, device_id=peer, device_id_type=MESH)

    pending = []

    def send(src, dst, ssem, rsem, device):
        copy = pltpu.make_async_remote_copy(
            src_ref=src, dst_ref=dst, send_sem=ssem, recv_sem=rsem, device_id=device, device_id_type=MESH
        )
        copy.start()
        pending.append(copy)

    def drain(kept=0):
        while len(pending) > kept:
            pending.pop(0).wait_send()

    def arrived(dst, ssem, rsem):
        pltpu.make_async_remote_copy(
            src_ref=dst, dst_ref=dst, send_sem=ssem, recv_sem=rsem, device_id=partner, device_id_type=MESH
        ).wait_recv()

    load_ids.wait()
    shifted = ids_ref[...] - me * CENT
    local = jnp.where(shifted < 0, shifted + K1, shifted)
    ones_row = jnp.ones((8, 128), BF16)
    load_sec.wait()
    table[...] = jnp.zeros_like(table)
    table[0, :, pl.ds(CENT, CENT)] = sec_ref[...].astype(F32)
    idbuf[x, :, pl.ds(0, CENT)] = sec_ref[...]
    idbuf[x, :, pl.ds(CENT, CENT)] = sec_ref[...]
    for j in range(BAND):
        rows = pl.ds(j * CENT, CENT)
        wanted = lax.broadcasted_iota(jnp.int32, (CENT, ROWS), 0) + j * CENT
        oh[rows, :] = jnp.where(local == wanted, 1.0, 0.0).astype(BF16)
        folded = oh[rows, pl.ds(0, 128)]
        for k in range(1, ROWS // 128):
            folded = folded + oh[rows, pl.ds(k * 128, 128)]
        table[j, :, pl.ds(0, CENT)] = dot_nt(ones_row, folded)[0:1]

    pl.semaphore_wait(barrier, len(peers))

    for d in reversed(near):
        kept = pl.ds(d, BAND - d) if d > 0 else pl.ds(0, BAND + d)
        t = d + BAND - 1
        send(table.at[kept], tables.at[t, kept], t_ss.at[t], t_rs.at[t], chip(d))
    for step in range(1, NX):
        send(idbuf.at[x], idbuf.at[x], id_ss.at[step - 1], id_rs.at[step - 1], xdev(step, c))

    def band(j):
        return pl.ds(j * CENT, CENT)

    def step_one(q):
        send(partb.at[band(2 * q + 1)], crecv.at[q], c_ss.at[q], c_rs.at[q], chip(1))

    def joined(j):
        arrived(crecv.at[j // 2], c_ss.at[j // 2], c_rs.at[j // 2])
        return part[band(j), :] + crecv[j // 2].astype(F32)

    def step_two(j):
        k = 4 + j // 4
        csend[k - 4] = joined(j).astype(BF16)
        send(csend.at[k - 4], crecv.at[k], c_ss.at[k], c_rs.at[k], chip(2))

    def received(k):
        arrived(crecv.at[k], c_ss.at[k], c_rs.at[k])
        return crecv[k].astype(F32)

    def step_three():
        csend[2] = (joined(4) + received(5)).astype(BF16)
        send(csend.at[2], crecv.at[6], c_ss.at[6], c_rs.at[6], chip(4))

    half = BAND // 2 * CENT
    load.wait()
    for begin in (half, 0):
        rows = pl.ds(begin, half)
        sums = jnp.dot(oh[rows, :], emb[...], preferred_element_type=F32)
        part[rows, :] = sums
        partb[rows, :] = sums.astype(BF16)

    step_one(3)
    step_one(1)
    step_one(2)
    step_one(0)
    for step in range(1, NX):
        arrived(idbuf.at[lax.rem(x + NX - step, NX)], id_ss.at[step - 1], id_rs.at[step - 1])
    lane = lax.broadcasted_iota(jnp.int32, (1, 128), 1)
    block = NY * NZ * 4
    quarter = NZ * 4
    group = lax.broadcasted_iota(jnp.int32, (block, 128), 0) + x * block
    hits = []
    for pair in range(NX // 2):
        names = jnp.where(lane < CENT, idbuf[2 * pair], idbuf[2 * pair + 1])
        hits.append(jnp.where(names == group, 1.0, 0.0))
    hit = (hits[0] + hits[1]).astype(BF16)
    ycsend[...] = jnp.zeros_like(ycsend)
    for k in range(NY):
        ycsend[k, :, pl.ds(0, CENT)] = dot_nt(ones_row, hit[k * quarter : (k + 1) * quarter])[0:1]
    for step in range(1, NY):
        to = lax.rem(y + step, NY)
        send(ycsend.at[to], ycrecv.at[step - 1], yc_ss.at[step - 1], yc_rs.at[step - 1], ydev(step, c))

    for d in near:
        kept = pl.ds(d, BAND - d) if d > 0 else pl.ds(0, BAND + d)
        t = d + BAND - 1
        arrived(tables.at[t, kept], t_ss.at[t], t_rs.at[t])
    totals, name_rows = [], []
    for j in range(BAND):
        total = table[j]
        for d in near:
            k = j + d
            if 0 <= k < BAND:
                total = total + tables[d + BAND - 1, k]
        totals.append(total)
        name_rows.append(table[0] if j == 0 else tables[BAND - 1 - j, 0])
    names, weights = [], []
    for k in range(BAND // 2):
        names.append(jnp.where(lane < CENT, pltpu.roll(name_rows[2 * k], CENT, 1), name_rows[2 * k + 1]))
        weights.append(1.0 / jnp.where(lane < CENT, totals[2 * k], pltpu.roll(totals[2 * k + 1], CENT, 1)))
    names = jnp.concatenate(names, axis=1).astype(jnp.int32)
    weights = jnp.concatenate(weights, axis=1)

    fold = HALF // 2
    far_x = [2, 1, 3, 0]
    far_y = [2, 1, 3, 0]
    for step in far_x:
        to = lax.rem(x + step, NX)
        wanted = lax.broadcasted_iota(jnp.int32, (block, BAND * CENT), 0) + to * block
        member = jnp.where(names == wanted, weights, 0.0).astype(BF16)
        sums = jnp.dot(member, partb[...], preferred_element_type=F32)
        for k in range(NY):
            apart[step, k] = sums[k * quarter : (k + 1) * quarter, :fold]
            bpart[k, to] = sums[k * quarter : (k + 1) * quarter, fold:]
        if step:
            asend[step - 1] = sums[:, :fold].reshape(NY, quarter, fold).astype(BF16)
            send(asend.at[step - 1], arecv.at[step - 1], a_ss.at[step - 1, 0], a_rs.at[step - 1, 0], xdev(step, c))
        for k in far_y:
            at = lax.rem(y + k, NY)
            if k:
                bsend[k - 1, step] = bpart[at, to].astype(BF16)
                send(
                    bsend.at[k - 1, step], brecv.at[k - 1, to],
                    b_ss.at[k - 1, step], b_rs.at[k - 1, to], ydev(k, c),
                )
    line = ycsend[y]
    for step in range(1, NY):
        arrived(ycrecv.at[step - 1], yc_ss.at[step - 1], yc_rs.at[step - 1])
        line = line + ycrecv[step - 1]
    zcsend[...] = line
    order = sorted(range(1, NZ), key=lambda step: -min(step, NZ - step))
    for step in order:
        send(zcsend, zcrecv.at[step - 1], zc_ss.at[step - 1], zc_rs.at[step - 1], zdev(step))
    step_two(6)

    old = len(pending)
    for t in range(NY):
        step = far_y[t]
        to = lax.rem(y + step, NY)
        sums = apart[0, to]
        for k in range(1, NX):
            if not t:
                arrived(arecv.at[k - 1], a_ss.at[k - 1, 0], a_rs.at[k - 1, 0])
            sums = sums + arecv[k - 1, to].astype(F32)
        if step:
            a2send[step - 1] = sums.astype(BF16)
            send(a2send.at[step - 1], a2recv.at[step - 1], a2_ss.at[step - 1], a2_rs.at[step - 1], ydev(step, c))
        else:
            first_half = sums
        step = far_x[t]
        to = lax.rem(x + step, NX)
        sums = bpart[y, to]
        for k in range(1, NY):
            arrived(brecv.at[k - 1, to], b_ss.at[k - 1, step], b_rs.at[k - 1, to])
            sums = sums + brecv[k - 1, to].astype(F32)
        if step:
            b2send[step - 1] = sums.astype(BF16)
            send(b2send.at[step - 1], b2recv.at[step - 1], b2_ss.at[step - 1], b2_rs.at[step - 1], xdev(step, c))
        else:
            second_half = sums
    step_two(2)
    for step in range(1, NY):
        arrived(a2recv.at[step - 1], a2_ss.at[step - 1], a2_rs.at[step - 1])
        first_half = first_half + a2recv[step - 1].astype(F32)
    for step in range(1, NX):
        arrived(b2recv.at[step - 1], b2_ss.at[step - 1], b2_rs.at[step - 1])
        second_half = second_half + b2recv[step - 1].astype(F32)

    for k in range(NZ // 2):
        zpart[2 * k] = first_half[8 * k : 8 * k + 8]
        zpart[2 * k + 1] = second_half[8 * k : 8 * k + 8]
    zsend[...] = zpart[...].astype(BF16)
    for step in order:
        to = lax.rem(z + step, NZ)
        send(zsend.at[to], zrecv.at[step - 1], z_ss.at[step - 1], z_rs.at[step - 1], zdev(step))

    step_three()
    counts = zcsend[...]
    for step in range(1, NZ):
        arrived(zcrecv.at[step - 1], zc_ss.at[step - 1], zc_rs.at[step - 1])
        counts = counts + zcrecv[step - 1]
    drain(len(pending) - old)
    eight = lax.broadcasted_iota(jnp.int32, (8, 128), 0) + (z // 2) * 8 == lax.broadcasted_iota(jnp.int32, (8, 128), 1)
    second_counts = jnp.sum(jnp.where(eight, counts, 0.0), axis=1, keepdims=True)
    sums = zpart[z]
    for step in reversed(order):
        arrived(zrecv.at[step - 1], z_ss.at[step - 1], z_rs.at[step - 1])
        sums = sums + zrecv[step - 1].astype(F32)
    second = (sums / second_counts).astype(BF16)
    pair, side = z // 2, lax.rem(z, 2)
    zg[pair, side] = second
    for step in order:
        send(zg.at[pair, side], zg.at[pair, side], za_ss.at[step - 1], za_rs.at[step - 1], zdev(step))
    scorer = y // (NY // 2)
    slot = lax.rem(y, NY // 2)
    eye = lax.broadcasted_iota(jnp.int32, (CENT, CENT), 0) == lax.broadcasted_iota(jnp.int32, (CENT, CENT), 1)
    count_column = jnp.sum(jnp.where(eye, totals[0][:, 0:CENT], 0.0), axis=1, keepdims=True)
    done = ((joined(0) + received(4) + received(6)) / count_column).astype(BF16)
    fc_out[...] = done
    xg[c, x] = done
    for step in range(1, NX):
        send(xg.at[c, x], xg.at[c, x], x_ss.at[step - 1], x_rs.at[step - 1], xdev(step, c))
    for d in (0, 1, 7, 2, 6, 3, 5, 4):
        there = lax.rem(pair + d, NZ // 2)
        for h in range(2):
            source = 2 * there + h
            step = lax.rem(z + NZ - source, NZ)
            if d:
                arrived(zg.at[there, h], za_ss.at[0], za_rs.at[step - 1])
        if not d:
            step = lax.rem(NZ + 2 * side - 1, NZ)
            arrived(zg.at[pair, 1 - side], za_ss.at[0], za_rs.at[step - 1])
            ours = zg[pair].astype(F32)
            for h in range(2):
                rows = jnp.where(side == 0, ours[h, 0:4], ours[h, 4:8])
                sc_out[:, pl.ds(h * fold, fold)] = rows.astype(BF16)
        for k in range(1, NY):
            send(zg.at[there], yg.at[c, slot, there], ya_ss.at[k - 1, d], ya_rs.at[c, slot], ydev(k, scorer))
    own_scorer = scorer == c
    to_scorer = pltpu.make_async_remote_copy(
        src_ref=zg, dst_ref=yg.at[c, slot], send_sem=pg_ss, recv_sem=ya_rs.at[c, slot],
        device_id=partner, device_id_type=MESH,
    )

    @pl.when(own_scorer)
    def _():
        yg[c, slot] = zg[...]

    @pl.when(jnp.logical_not(own_scorer))
    def _():
        to_scorer.start()

    for step in range(1, NX):
        source = lax.rem(x + NX - step, NX)
        arrived(xg.at[c, source], x_ss.at[step - 1], x_rs.at[step - 1])
    send(xg.at[c], xg.at[c], pt_ss, pt_rs, partner)
    arrived(xg.at[1 - c], pt_ss, pt_rs)
    for s in range(NY // 2):
        for k in range(2):
            here = jnp.logical_and(c * (NY // 2) + s == y, c == k)

            @pl.when(jnp.logical_not(here))
            def _():
                arrived(yg.at[k, s], pg_ss, ya_rs.at[k, s])

    groups = NY // 2 * quarter
    scores = jnp.zeros((NX * CENT, groups), F32)
    squares = jnp.zeros((groups, 1), F32)
    for k in range(2):
        for h in range(2):
            b = yg[k, :, :, h].reshape(groups, fold)
            scores = scores + dot_nt(xg[k, :, :, pl.ds(h * fold, fold)].reshape(NX * CENT, fold), b)
            b32 = b.astype(F32)
            squares = squares + jnp.sum(b32 * b32, axis=1, keepdims=True)
    eye = lax.broadcasted_iota(jnp.int32, (groups, groups), 0) == lax.broadcasted_iota(jnp.int32, (groups, groups), 1)
    norm_row = jnp.sum(jnp.where(eye, squares, 0.0), axis=0, keepdims=True)
    ssend[...] = (scores - 0.5 * norm_row).astype(BF16).reshape(NX, CENT, groups)
    holder = x // (NX // 2)
    out_slot = lax.rem(x, NX // 2) * 2 + c
    for step in range(1, NX):
        to = lax.rem(x + step, NX)
        send(ssend.at[to], sret.at[out_slot], r_ss.at[step], r_rs.at[out_slot], xdev(step, holder))
    own_holder = holder == c
    to_holder = pltpu.make_async_remote_copy(
        src_ref=ssend.at[x], dst_ref=sret.at[out_slot], send_sem=r_ss.at[0], recv_sem=r_rs.at[out_slot],
        device_id=partner, device_id_type=MESH,
    )

    @pl.when(own_holder)
    def _():
        sret[out_slot] = ssend[x]

    @pl.when(jnp.logical_not(own_holder))
    def _():
        to_holder.start()

    drain()

    @pl.when(jnp.logical_not(own_scorer))
    def _():
        to_scorer.wait_send()

    @pl.when(jnp.logical_not(own_holder))
    def _():
        to_holder.wait_send()

    for s in range(NX):
        here = jnp.logical_and(c * (NX // 2) + s // 2 == x, c == s % 2)

        @pl.when(jnp.logical_not(here))
        def _():
            arrived(sret.at[s], r_ss.at[0], r_rs.at[s])


def write_out(fc, sc, sret, fc_out, sc_out, scores_out, wide, sems):
    copies = [
        pltpu.make_async_copy(fc, fc_out, sems.at[0]),
        pltpu.make_async_copy(sc, sc_out, sems.at[1]),
    ]
    for copy in copies:
        copy.start()
    groups = sret.shape[2]
    for s in range(NX):
        wide[:, pl.ds(s * groups, groups)] = sret[s].astype(F32)
    copies.append(pltpu.make_async_copy(wide, scores_out, sems.at[2]))
    copies[2].start()
    for copy in copies:
        copy.wait()


def shards(embeddings, first_level, second_level):
    dma = pltpu.SemaphoreType.DMA
    quarter = NZ * 4
    groups = NY // 2 * quarter
    fold = HALF // 2
    vmem = pl.BlockSpec(memory_space=pltpu.VMEM)
    hbm = pl.BlockSpec(memory_space=pltpu.HBM)
    operands = (embeddings, first_level.reshape(1, ROWS), second_level.reshape(1, CENT))
    first, second, returned = pl.pallas_call(
        kernel,
        out_shape=(
            jax.ShapeDtypeStruct((CENT, HALF), BF16),
            jax.ShapeDtypeStruct((4, HALF), BF16),
            jax.ShapeDtypeStruct((NX, CENT, groups), BF16),
        ),
        in_specs=[hbm] * 3,
        out_specs=(vmem,) * 3,
        scratch_shapes=[
            pltpu.VMEM((1, ROWS), jnp.int32),
            pltpu.VMEM((1, CENT), jnp.int32),
            pltpu.VMEM((ROWS, HALF), BF16),
            pltpu.VMEM((BAND * CENT, ROWS), BF16),
            pltpu.VMEM((BAND * CENT, HALF), F32),
            pltpu.VMEM((BAND * CENT, HALF), BF16),
            pltpu.VMEM((3, CENT, HALF), BF16),
            pltpu.VMEM((BAND - 1, CENT, HALF), BF16),
            pltpu.VMEM((BAND, 1, 128), F32),
            pltpu.VMEM((2 * BAND - 1, BAND, 1, 128), F32),
            pltpu.VMEM((2, NX, CENT, HALF), BF16),
            pltpu.VMEM((NX, 1, 128), jnp.int32),
            pltpu.VMEM((NX - 1, NY, quarter, fold), BF16),
            pltpu.VMEM((NX - 1, NY, quarter, fold), BF16),
            pltpu.VMEM((NX, NY, quarter, fold), F32),
            pltpu.VMEM((NY - 1, NX, quarter, fold), BF16),
            pltpu.VMEM((NY - 1, NX, quarter, fold), BF16),
            pltpu.VMEM((NY, NX, quarter, fold), F32),
            pltpu.VMEM((NY - 1, quarter, fold), BF16),
            pltpu.VMEM((NY - 1, quarter, fold), BF16),
            pltpu.VMEM((NX - 1, quarter, fold), BF16),
            pltpu.VMEM((NX - 1, quarter, fold), BF16),
            pltpu.VMEM((NY, 1, 128), F32),
            pltpu.VMEM((NY - 1, 1, 128), F32),
            pltpu.VMEM((1, 128), F32),
            pltpu.VMEM((NZ - 1, 1, 128), F32),
            pltpu.VMEM((NZ, 8, fold), BF16),
            pltpu.VMEM((NZ, 8, fold), F32),
            pltpu.VMEM((NZ - 1, 8, fold), BF16),
            pltpu.VMEM((NZ // 2, 2, 8, fold), BF16),
            pltpu.VMEM((2, NY // 2, NZ // 2, 2, 8, fold), BF16),
            pltpu.VMEM((NX, CENT, groups), BF16),
            dma, dma, dma,
            dma((2 * BAND - 1,)), dma((2 * BAND - 1,)),
            dma((BAND - 1,)), dma((BAND - 1,)),
            dma((NX - 1,)), dma((NX - 1,)),
            dma((NX - 1,)), dma((NX - 1,)),
            dma, dma,
            dma((NX - 1, NY)), dma((NX - 1, NY)),
            dma((NY - 1, NX)), dma((NY - 1, NX)),
            dma((NY - 1,)), dma((NY - 1,)),
            dma((NX - 1,)), dma((NX - 1,)),
            dma((NY - 1,)), dma((NY - 1,)),
            dma((NZ - 1,)), dma((NZ - 1,)),
            dma((NZ - 1,)), dma((NZ - 1,)),
            dma((NZ - 1,)), dma((NZ - 1,)),
            dma((NY - 1, NZ // 2)), dma((2, NY // 2)), dma,
            dma((NX,)), dma((NX,)),
        ],
        compiler_params=pltpu.CompilerParams(
            collective_id=0, has_side_effects=True, vmem_limit_bytes=40 << 20
        ),
        name="update",
    )(*(pltpu.with_memory_space_constraint(a, pltpu.HBM) for a in operands))
    return pl.pallas_call(
        write_out,
        out_shape=(
            jax.ShapeDtypeStruct((CENT, HALF), BF16),
            jax.ShapeDtypeStruct((4, HALF), BF16),
            jax.ShapeDtypeStruct((CENT, HALF), F32),
        ),
        in_specs=[vmem] * 3,
        out_specs=(hbm,) * 3,
        scratch_shapes=[pltpu.VMEM((CENT, HALF), F32), dma((3,))],
        compiler_params=pltpu.CompilerParams(vmem_limit_bytes=8 << 20),
        name="write_out",
    )(first, second, returned)


def solution(mesh):
    torus = Mesh(mesh.devices.reshape(NX, NY, NZ, mesh.shape["mp"]), (*DP, "mp"))
    return jax.shard_map(
        shards,
        mesh=torus,
        in_specs=(P(DP, "mp"), P(DP), P(DP, None)),
        out_specs=(P(DP, "mp"), P(DP, "mp"), P(DP, "mp")),
        check_vma=False,
    )
```
